32 devices in a mesh: groups: 2 (over x), seq: 16 (over z, y, core).
Axes of the slice: x: 2, y: 2, z: 4, core: 2. Of those that a mesh axis runs over, the one named last changes fastest.
Arguments:
- queries: bfloat16 [64, 4, 8192], P(('groups', 'seq')), parts along dimension 0, may hold values from -128 to 128
- step_keys: bfloat16 [64, 4, 1024], P(('groups', 'seq')), parts along dimension 0, may hold values from -15 to 15
- step_values: bfloat16 [64, 4, 1024], P(('groups', 'seq')), parts along dimension 0, may hold values from -48 to 48
- sample_keys: bfloat16 [64, 1024, 1024], P(('groups', 'seq')), parts along dimension 0, may hold values from -6 to 6
- sample_values: bfloat16 [64, 1024, 1024], P(('groups', 'seq')), parts along dimension 0, may hold values from -48 to 48
- suffix_len: int32 [64], P(('groups', 'seq')), parts along dimension 0, may hold values from 128 to 1024
- prompt_id: int32 [64], P(('groups', 'seq')), parts along dimension 0, may hold values from 0 to 1, as said below
- document_keys: bfloat16 [4, 4096, 1024], P('groups', 'seq'), parts along dimension 0, may hold values from -6 to 6
- document_values: bfloat16 [4, 4096, 1024], P('groups', 'seq'), parts along dimension 0, may hold values from -48 to 48
Outputs:
- attended: bfloat16 [64, 4, 8192], P(('groups', 'seq')), parts along dimension 0
The draws below stay inside these ranges and needn't reach their ends.
There are 2 independent parts, one for each index of `groups`. The reference program is written for one: setup_inputs(seed, part) draws one part's arguments, and reference() takes and returns one part's arrays. A program takes and returns all parts, laid end to end along the dimension named above; each array names one. Nothing has to cross between parts.
Inputs may be any that keep to these rules, and one draw needn't show every extreme that they name: `prompt_id`: each prompt id is held by exactly 16 samples.
All inputs are finite; a program needn't handle non-finite values.
Results may differ from the reference program's by a relative error of at most 0.0013.
Values may be sent and summed in bfloat16 or wider, within the bound.
No kernel may reach another device: no remote copies, remote signals or barrier semaphores. Data moves between devices by JAX's collectives and lax.ppermute only.
A program may use at most 192 MiB of HBM per device.

```python
import jax
import jax.numpy as jnp
from jax import lax

QUERY_HEADS = 64
KEY_VALUE_HEADS = 8
HEAD_SIZE = 128
GROUP_PROMPTS = 2
DECODE_STEPS = 4
BLOCK_PREFIX = 256
SUFFIX_SLOTS = 1024
GROUP_SAMPLES = 32
PREFIX_LENGTH = 4096


def draw_queries(key, part):
    leading_key = jax.random.fold_in(jax.random.fold_in(key, 101), 0)
    entry_list = jnp.clip(2.0 * jax.random.normal(leading_key, (GROUP_SAMPLES, DECODE_STEPS, QUERY_HEADS, HEAD_SIZE), jnp.float32), -12.0, 12.0)
    return entry_list.reshape(GROUP_SAMPLES, DECODE_STEPS, QUERY_HEADS * HEAD_SIZE).astype(jnp.bfloat16)


def draw_document_keys(key, part):
    leading_key = jax.random.fold_in(key, 202)
    entry_list = jnp.clip(jax.random.normal(leading_key, (GROUP_PROMPTS, PREFIX_LENGTH, KEY_VALUE_HEADS, HEAD_SIZE), jnp.float32), -6.0, 6.0)
    return entry_list.reshape(GROUP_PROMPTS, PREFIX_LENGTH, KEY_VALUE_HEADS * HEAD_SIZE).astype(jnp.bfloat16)


def draw_prompt_id(key, part):
    shuffled = jax.random.permutation(jax.random.fold_in(key, 303), GROUP_SAMPLES)
    return (shuffled // (GROUP_SAMPLES // GROUP_PROMPTS)).astype(jnp.int32)


def with_ends(entries, key, low, high):
    spot = [jax.random.randint(jax.random.fold_in(key, axis), (), 0, length) for axis, length in enumerate(entries.shape)]
    widest = entries.shape.index(max(entries.shape))
    beside = spot[:widest] + [(spot[widest] + 1) % entries.shape[widest]] + spot[widest + 1:]
    return entries.at[tuple(spot)].set(low).at[tuple(beside)].set(high)


def block_scale(stream_key, dims, cuts, least, top_value):
    loudness = 1.0
    for dim, parts in cuts:
        draws = jax.random.uniform(jax.random.fold_in(jax.random.fold_in(stream_key, 6), dim), (parts,), jnp.float32, least / len(cuts), top_value / len(cuts))
        loudness = loudness * jnp.repeat(jnp.exp(draws), dims[dim] // parts).reshape((-1,) + (1,) * (len(dims) - 1 - dim))
    return loudness


def centred(own_key, extent, scale, most, cuts=(), held_as=jnp.bfloat16):
    result = jax.random.normal(own_key, extent, jnp.float32) * scale
    if len(cuts) > 0:
        result = block_scale(own_key, extent, cuts, -0.22, 0.18) * result
    return jnp.clip(result, min=-most, max=most).astype(held_as)


def setup_inputs(seed: int = 0, part: int = 0) -> dict:
    keys = jax.random.split(jax.random.key(seed), 10)
    part_splits = jax.random.split(jax.random.fold_in(keys[9], part), 10)
    queries = draw_queries(jax.random.fold_in(jax.random.fold_in(keys[9], part), 71), part)
    step_keys = centred(part_splits[1], (GROUP_SAMPLES, DECODE_STEPS, KEY_VALUE_HEADS * HEAD_SIZE), 2.5, 15.0, ((0, 16),))
    step_values = centred(part_splits[2], (GROUP_SAMPLES, DECODE_STEPS, KEY_VALUE_HEADS * HEAD_SIZE), 8.0, 48.0, ((0, 16),))
    sample_keys = centred(part_splits[3], (GROUP_SAMPLES, SUFFIX_SLOTS, KEY_VALUE_HEADS * HEAD_SIZE), 1.0, 6.0, ((0, 16),))
    sample_values = centred(part_splits[4], (GROUP_SAMPLES, SUFFIX_SLOTS, KEY_VALUE_HEADS * HEAD_SIZE), 8.0, 48.0, ((0, 16),))
    suffix_len = with_ends(jax.random.randint(part_splits[5], (GROUP_SAMPLES,), SUFFIX_SLOTS // 8, SUFFIX_SLOTS + 1), jax.random.fold_in(part_splits[5], 1), SUFFIX_SLOTS // 8, SUFFIX_SLOTS).astype(jnp.int32)
    prompt_id = draw_prompt_id(jax.random.fold_in(jax.random.fold_in(keys[9], part), 71), part)
    document_keys = draw_document_keys(jax.random.fold_in(jax.random.fold_in(keys[9], part), 71), part)
    document_values = centred(part_splits[8], (GROUP_PROMPTS, PREFIX_LENGTH, KEY_VALUE_HEADS * HEAD_SIZE), 8.0, 48.0, ((1, 16),))
    return dict(queries=queries, step_keys=step_keys, step_values=step_values, sample_keys=sample_keys, sample_values=sample_values, suffix_len=suffix_len, prompt_id=prompt_id, document_keys=document_keys, document_values=document_values)


def rounded(values):
    return lax.optimization_barrier(values.astype(jnp.bfloat16)).astype(jnp.float32)


def reference(queries, step_keys, step_values, sample_keys, sample_values, suffix_len, prompt_id, document_keys, document_values):
    group_count = QUERY_HEADS // KEY_VALUE_HEADS
    block_list = PREFIX_LENGTH // BLOCK_PREFIX
    scaling = HEAD_SIZE ** -0.5

    def per_sample(members):
        query_vector, recent_key_rows, recent_value_rows, cache_key_rows, cache_value_rows, length, prompt_row = members
        query_matrix = query_vector.astype(jnp.float32).reshape(DECODE_STEPS, KEY_VALUE_HEADS, group_count, HEAD_SIZE)
        present_keys = lax.dynamic_index_in_dim(document_keys, prompt_row, 0, keepdims=False)
        present_values = lax.dynamic_index_in_dim(document_values, prompt_row, 0, keepdims=False)
        present_keys = present_keys.astype(jnp.float32).reshape(block_list, BLOCK_PREFIX, KEY_VALUE_HEADS, HEAD_SIZE)
        present_values = present_values.astype(jnp.float32).reshape(block_list, BLOCK_PREFIX, KEY_VALUE_HEADS, HEAD_SIZE)
        prefix_score = jnp.einsum('tgrd,bkgd->btgrk', query_matrix, present_keys) * scaling
        prefix_max = jnp.max(prefix_score, axis=-1)
        prefix_exp = jnp.exp(prefix_score - prefix_max[..., None])
        prefix_total = jnp.sum(prefix_exp, axis=-1)
        prefix_out = jnp.einsum('btgrk,bkgd->btgrd', rounded(prefix_exp), present_values)

        cached_key_set = cache_key_rows.astype(jnp.float32).reshape(SUFFIX_SLOTS, KEY_VALUE_HEADS, HEAD_SIZE)
        cached_value_set = cache_value_rows.astype(jnp.float32).reshape(SUFFIX_SLOTS, KEY_VALUE_HEADS, HEAD_SIZE)
        recent_keys = recent_key_rows.astype(jnp.float32).reshape(DECODE_STEPS, KEY_VALUE_HEADS, HEAD_SIZE)
        recent_values = recent_value_rows.astype(jnp.float32).reshape(DECODE_STEPS, KEY_VALUE_HEADS, HEAD_SIZE)
        cache_score = jnp.einsum('tgrd,kgd->tgrk', query_matrix, cached_key_set) * scaling
        fresh_score = jnp.einsum('tgrd,ugd->tgru', query_matrix, recent_keys) * scaling
        cache_live = (jnp.arange(SUFFIX_SLOTS, dtype=jnp.int32) < length)[None, None, None, :]
        fresh_live = (jnp.arange(DECODE_STEPS)[None, :] <= jnp.arange(DECODE_STEPS)[:, None])[:, None, None, :]
        suffix_max = jnp.maximum(jnp.max(jnp.where(cache_live, cache_score, -jnp.inf), axis=-1),
                                 jnp.max(jnp.where(fresh_live, fresh_score, -jnp.inf), axis=-1))
        cache_exp = jnp.where(cache_live, jnp.exp(cache_score - suffix_max[..., None]), 0.0)
        fresh_exp = jnp.where(fresh_live, jnp.exp(fresh_score - suffix_max[..., None]), 0.0)
        suffix_total = jnp.sum(cache_exp, axis=-1) + jnp.sum(fresh_exp, axis=-1)
        suffix_out = (jnp.einsum('tgrk,kgd->tgrd', rounded(cache_exp), cached_value_set)
                      + jnp.einsum('tgru,ugd->tgrd', rounded(fresh_exp), recent_values))

        highest = jnp.maximum(jnp.max(prefix_max, axis=0), suffix_max)
        prefix_scale = jnp.exp(prefix_max - highest[None])
        suffix_scale = jnp.exp(suffix_max - highest)
        numerator = jnp.sum(prefix_out * prefix_scale[..., None], axis=0) + suffix_out * suffix_scale[..., None]
        denominator = jnp.sum(prefix_total * prefix_scale, axis=0) + suffix_total * suffix_scale
        return (numerator / denominator[..., None]).reshape(DECODE_STEPS, QUERY_HEADS * HEAD_SIZE).astype(jnp.bfloat16)

    return lax.map(per_sample, (queries, step_keys, step_values, sample_keys, sample_values, suffix_len, prompt_id))
```

```python
import functools

import jax
import jax.numpy as jnp
from jax import lax
from jax.experimental import pallas as pl
from jax.experimental.pallas import tpu as pltpu
from jax.sharding import PartitionSpec as P

QUERY_HEADS = 64
KEY_VALUE_HEADS = 8
HEAD_SIZE = 128
GROUP = QUERY_HEADS // KEY_VALUE_HEADS
SCALING = HEAD_SIZE ** (-0.5)
LANES = 128
PARTNER_ORDER = (6, 7, 4, 2, 5, 3, 1)


def whole(space=pltpu.VMEM):
    return pl.BlockSpec(memory_space=space)


def slice_kernel(partners, keys_ref, values_ref, *refs):
    out_refs, sem = refs[:-1], refs[-1]
    mine = lax.axis_index("seq") % KEY_VALUE_HEADS
    copies = []
    for slot, partner in enumerate(partners):
        head = jnp.bitwise_xor(mine, partner)
        columns = pl.ds(pl.multiple_of(head * HEAD_SIZE, HEAD_SIZE), HEAD_SIZE)
        for side, source in enumerate((keys_ref, values_ref)):
            copy = pltpu.make_async_copy(
                source.at[:, :, columns], out_refs[slot].at[side], sem.at[slot, side]
            )
            copy.start()
            copies.append(copy)
    for copy in copies:
        copy.wait()


def head_slices(keys, values, partners):
    prompts, block, _ = keys.shape
    piece = jax.ShapeDtypeStruct((2, prompts, block, HEAD_SIZE), keys.dtype)
    return pl.pallas_call(
        functools.partial(slice_kernel, partners),
        out_shape=[piece] * len(partners),
        in_specs=[whole(pl.ANY)] * 2,
        out_specs=[whole(pl.ANY)] * len(partners),
        scratch_shapes=[pltpu.SemaphoreType.DMA((len(partners), 2))],
        name="head_slices",
    )(keys, values)


def pack_kernel(ids_ref, queries_ref, out_ref):
    owned, steps, _ = queries_ref.shape
    rows = owned * steps * GROUP
    lane = lax.broadcasted_iota(jnp.int32, (out_ref.shape[1] - rows, LANES), 1)
    marks = jnp.zeros(lane.shape, jnp.float32)
    for n in range(owned):
        marks = jnp.where(lane == n, ids_ref[n].astype(jnp.float32), marks)
    marks = marks.astype(jnp.bfloat16)
    for head in range(KEY_VALUE_HEADS):
        parts = []
        for n in range(owned):
            for r in range(GROUP):
                first = (head * GROUP + r) * HEAD_SIZE
                parts.append(queries_ref[n, :, first : first + HEAD_SIZE].astype(jnp.float32))
        block = jnp.concatenate(parts, axis=0).astype(jnp.bfloat16)
        for copy in range(out_ref.shape[0] // KEY_VALUE_HEADS):
            out_ref[copy * KEY_VALUE_HEADS + head, :rows, :] = block
            out_ref[copy * KEY_VALUE_HEADS + head, rows:, :] = marks


def pack_queries(queries, prompt_id, device_count):
    owned, steps, _ = queries.shape
    rows = owned * steps * GROUP
    return pl.pallas_call(
        pack_kernel,
        out_shape=jax.ShapeDtypeStruct((device_count, rows + 16, HEAD_SIZE), jnp.bfloat16),
        in_specs=[whole(pltpu.SMEM), whole()],
        out_specs=whole(),
        name="pack_queries",
    )(prompt_id, queries)


def contract(left, right, dims):
    return lax.dot_general(left, right, (dims, ((), ())), preferred_element_type=jnp.float32)


def diagonal_row(columns):
    row = lax.broadcasted_iota(jnp.int32, columns.shape, 0)
    lane = lax.broadcasted_iota(jnp.int32, columns.shape, 1)
    return jnp.sum(jnp.where(lane % columns.shape[0] == row, columns, 0.0), axis=0, keepdims=True)


def max_and_total(peak, total):
    rows = peak.shape[0]
    lane = lax.broadcasted_iota(jnp.int32, (rows, LANES), 1)
    return jnp.where(lane < LANES // 2, peak, total)


def suffix_kernel(len_ref, query_ref, keys_ref, values_ref, new_keys_ref, new_values_ref, out_ref, aux_ref):
    owned, slots, _ = keys_ref.shape
    steps = new_keys_ref.shape[1]
    rows = steps * GROUP
    aux_parts = []
    for n in range(owned):
        query = query_ref[0, n * rows : (n + 1) * rows, :]
        cache = contract(query, keys_ref[n], ((1,), (1,))) * SCALING
        fresh = contract(query, new_keys_ref[n], ((1,), (1,))) * SCALING
        cache_live = lax.broadcasted_iota(jnp.int32, cache.shape, 1) < len_ref[n]
        fresh_live = (
            lax.broadcasted_iota(jnp.int32, fresh.shape, 1)
            <= lax.broadcasted_iota(jnp.int32, fresh.shape, 0) % steps
        )
        peak = jnp.maximum(
            jnp.max(jnp.where(cache_live, cache, -jnp.inf), axis=1, keepdims=True),
            jnp.max(jnp.where(fresh_live, fresh, -jnp.inf), axis=1, keepdims=True),
        )
        cache_exp = jnp.where(cache_live, jnp.exp(cache - peak), 0.0)
        fresh_exp = jnp.where(fresh_live, jnp.exp(fresh - peak), 0.0)
        total = jnp.sum(cache_exp, axis=1, keepdims=True) + jnp.sum(fresh_exp, axis=1, keepdims=True)
        out = contract(cache_exp.astype(jnp.bfloat16), values_ref[n], ((1,), (0,))) + contract(
            fresh_exp.astype(jnp.bfloat16), new_values_ref[n], ((1,), (0,))
        )
        out_ref[0, n * rows : (n + 1) * rows, :] = out
        aux_parts.append(max_and_total(peak, total))
    aux_ref[0] = diagonal_row(jnp.concatenate(aux_parts, axis=0))


def suffix_part(suffix_len, packed, keys, values, new_keys, new_values):
    owned, slots, _ = keys.shape
    steps = new_keys.shape[1]
    rows = owned * steps * GROUP
    return pl.pallas_call(
        suffix_kernel,
        grid_spec=pltpu.PrefetchScalarGridSpec(
            num_scalar_prefetch=1,
            grid=(KEY_VALUE_HEADS,),
            in_specs=[
                pl.BlockSpec((1, packed.shape[1], HEAD_SIZE), lambda h, _: (h, 0, 0)),
                pl.BlockSpec((owned, slots, HEAD_SIZE), lambda h, _: (0, 0, h)),
                pl.BlockSpec((owned, slots, HEAD_SIZE), lambda h, _: (0, 0, h)),
                pl.BlockSpec((owned, steps, HEAD_SIZE), lambda h, _: (0, 0, h)),
                pl.BlockSpec((owned, steps, HEAD_SIZE), lambda h, _: (0, 0, h)),
            ],
            out_specs=[
                pl.BlockSpec((1, rows, HEAD_SIZE), lambda h, _: (h, 0, 0)),
                pl.BlockSpec((1, 1, LANES), lambda h, _: (h, 0, 0)),
            ],
        ),
        out_shape=[
            jax.ShapeDtypeStruct((KEY_VALUE_HEADS, rows, HEAD_SIZE), jnp.float32),
            jax.ShapeDtypeStruct((KEY_VALUE_HEADS, 1, LANES), jnp.float32),
        ],
        name="suffix_part",
    )(suffix_len, packed, keys, values, new_keys, new_values)


def prefix_kernel(rows, chunk, ids_ref, queries_ref, *refs):
    pieces = refs[:KEY_VALUE_HEADS]
    out_ref, query_scratch, out_scratch, aux_scratch, place_ref, count_ref = refs[KEY_VALUE_HEADS:]
    samples = ids_ref.shape[0]
    devices = queries_ref.shape[0]
    owned = samples // devices
    prompts = pieces[0].shape[1]
    per_prompt = samples // prompts
    for p in range(prompts):
        count_ref[p] = 0

    def sort_one(device, carry):
        for n in range(owned):
            prompt = ids_ref[device * owned + n]
            rank = count_ref[prompt]
            count_ref[prompt] = rank + 1
            place = prompt * per_prompt + rank
            place_ref[device * owned + n] = place
            target = pl.ds(pl.multiple_of(place * rows, rows), rows)
            query_scratch[target, :] = queries_ref[device, n * rows : (n + 1) * rows, :]
        return carry

    lax.fori_loop(0, devices, sort_one, 0)
    chunks = per_prompt * rows // chunk

    def attend(step, carry):
        prompt = step // chunks
        target = pl.ds(pl.multiple_of(step * chunk, chunk), chunk)
        query = query_scratch[target, :]
        best = mass = acc = None
        for piece in pieces:
            score = contract(query, piece[0, prompt], ((1,), (1,))) * SCALING
            peak = jnp.max(score, axis=1, keepdims=True)
            weight = jnp.exp(score - peak)
            total = jnp.sum(weight, axis=1, keepdims=True)
            part = contract(weight.astype(jnp.bfloat16), piece[1, prompt], ((1,), (0,)))
            if best is None:
                best, mass, acc = peak, total, part
            else:
                top = jnp.maximum(best, peak)
                old = jnp.exp(best - top)
                new = jnp.exp(peak - top)
                acc = acc * old + part * new
                mass = mass * old + total * new
                best = top
        out_scratch[target, :] = acc
        aux_scratch[target, :] = max_and_total(best, mass)
        return carry

    lax.fori_loop(0, prompts * chunks, attend, 0)

    def emit(device, carry):
        aux_parts = []
        for n in range(owned):
            place = place_ref[device * owned + n]
            source = pl.ds(pl.multiple_of(place * rows, rows), rows)
            out_ref[device, n * rows : (n + 1) * rows, :] = out_scratch[source, :]
            aux_parts.append(aux_scratch[source, :])
        row = diagonal_row(jnp.concatenate(aux_parts, axis=0))
        out_ref[device, owned * rows :, :] = jnp.broadcast_to(row, (8, LANES))
        return carry

    lax.fori_loop(0, devices, emit, 0)


def prefix_part(ids, queries, pieces, rows):
    devices = queries.shape[0]
    samples = ids.shape[0]
    owned = samples // devices
    prompts = pieces[0].shape[1]
    chunk = min(256, samples * rows // prompts)
    return pl.pallas_call(
        functools.partial(prefix_kernel, rows, chunk),
        out_shape=jax.ShapeDtypeStruct((devices, owned * rows + 8, HEAD_SIZE), jnp.float32),
        in_specs=[whole(pltpu.SMEM)] + [whole()] * (1 + len(pieces)),
        out_specs=whole(),
        scratch_shapes=[
            pltpu.VMEM((samples * rows, HEAD_SIZE), jnp.bfloat16),
            pltpu.VMEM((samples * rows, HEAD_SIZE), jnp.float32),
            pltpu.VMEM((samples * rows, HEAD_SIZE), jnp.float32),
            pltpu.SMEM((samples,), jnp.int32),
            pltpu.SMEM((prompts,), jnp.int32),
        ],
        name="prefix_part",
    )(ids, queries, *pieces)


def merge_kernel(got_ref, local_ref, local_aux_ref, out_ref):
    owned, steps, _ = out_ref.shape
    rows = local_ref.shape[1]
    half = LANES // 2
    groups = got_ref.shape[0] // KEY_VALUE_HEADS
    aux = [local_aux_ref[:, 0, :]]
    for g in range(groups):
        aux.append(
            jnp.concatenate(
                [got_ref[g * KEY_VALUE_HEADS + h, rows : rows + 1, :] for h in range(KEY_VALUE_HEADS)],
                axis=0,
            )
        )
    peaks = [a[:, :half] for a in aux]
    totals = [a[:, half:] for a in aux]
    highest = functools.reduce(jnp.maximum, peaks)
    scales = [jnp.exp(peak - highest) for peak in peaks]
    denominator = functools.reduce(jnp.add, [t * s for t, s in zip(totals, scales)])
    factors = [jnp.transpose(s / denominator) for s in scales]
    for h in range(KEY_VALUE_HEADS):
        result = local_ref[h] * factors[0][:, h : h + 1]
        for g in range(groups):
            result += got_ref[g * KEY_VALUE_HEADS + h, :rows, :] * factors[g + 1][:, h : h + 1]
        for n in range(owned):
            for r in range(GROUP):
                first = (h * GROUP + r) * HEAD_SIZE
                start = (n * GROUP + r) * steps
                out_ref[n, :, first : first + HEAD_SIZE] = result[start : start + steps, :].astype(
                    jnp.bfloat16
                )


def merge(got, local, local_aux, shape):
    return pl.pallas_call(
        merge_kernel,
        out_shape=jax.ShapeDtypeStruct(shape, jnp.bfloat16),
        in_specs=[whole()] * 3,
        out_specs=whole(),
        name="merge",
    )(got, local, local_aux)


def body(
    queries,
    step_keys,
    step_values,
    sample_keys,
    sample_values,
    suffix_len,
    prompt_id,
    document_keys,
    document_values,
):
    owned, steps, _ = queries.shape
    devices = lax.axis_size("seq")
    rows = steps * GROUP
    assert 2 * owned * rows == LANES and devices % KEY_VALUE_HEADS == 0
    sliced = head_slices(document_keys, document_values, PARTNER_ORDER + (0,))
    pieces = [sliced[-1]]
    for partner, piece in zip(PARTNER_ORDER, sliced):
        route = [(i, i ^ partner) for i in range(devices)]
        pieces.append(lax.ppermute(piece, "seq", route))
    packed = pack_queries(queries, prompt_id, devices)
    head_queries = lax.all_to_all(packed, "seq", split_axis=0, concat_axis=0, tiled=True)
    head_ids = head_queries[:, owned * rows, :owned].reshape(-1).astype(jnp.int32)
    local, local_aux = suffix_part(
        suffix_len, packed, sample_keys, sample_values, step_keys, step_values
    )
    sent = prefix_part(head_ids, head_queries, pieces, rows)
    got = lax.all_to_all(sent, "seq", split_axis=0, concat_axis=0, tiled=True)
    return merge(got, local, local_aux, queries.shape)


def solution(mesh):
    shared = P(("groups", "seq"), None, None)
    split = P("groups", "seq", None)
    return jax.shard_map(
        body,
        mesh=mesh,
        in_specs=(shared,) * 5 + (P(("groups", "seq")),) * 2 + (split,) * 2,
        out_specs=shared,
        check_vma=False,
    )
```

```python
import functools
import math

import jax
import jax.numpy as jnp
from jax import lax
from jax.experimental import pallas as pl
from jax.experimental.pallas import tpu as pltpu
from jax.sharding import PartitionSpec as P


QUERY_HEADS = 64
KEY_VALUE_HEADS = 8
HEAD_SIZE = 128
GROUP = QUERY_HEADS // KEY_VALUE_HEADS
SCALING = HEAD_SIZE ** (-0.5)
LANES = 128
EARLY = (6, 7)
LATE = (4, 2, 5, 3, 1)
LIMIT = pltpu.CompilerParams(vmem_limit_bytes=24 * 1024 * 1024)
WEIGHT_SCALE = SCALING * math.log2(math.e)


def whole(space=pltpu.VMEM):
    return pl.BlockSpec(memory_space=space)


def near(array):
    return pltpu.with_memory_space_constraint(array, pltpu.VMEM)


def far(array):
    return pltpu.with_memory_space_constraint(array, pltpu.HBM)


def slice_kernel(partners, keys_ref, values_ref, *refs):
    out_refs, sem = refs[:-1], refs[-1]
    mine = lax.axis_index("seq") % KEY_VALUE_HEADS
    copies = []
    for slot, partner in enumerate(partners):
        head = jnp.bitwise_xor(mine, partner)
        columns = pl.ds(pl.multiple_of(head * HEAD_SIZE, HEAD_SIZE), HEAD_SIZE)
        for side, source in enumerate((keys_ref, values_ref)):
            copy = pltpu.make_async_copy(
                source.at[:, :, columns], out_refs[slot].at[side], sem.at[slot, side]
            )
            copy.start()
            copies.append(copy)
    for copy in copies:
        copy.wait()


def head_slices(keys, values, partners):
    prompts, block, _ = keys.shape
    piece = jax.ShapeDtypeStruct((2, prompts, block, HEAD_SIZE), keys.dtype)
    pieces = pl.pallas_call(
        functools.partial(slice_kernel, partners),
        out_shape=[piece] * len(partners),
        in_specs=[whole(pltpu.HBM)] * 2,
        out_specs=[whole()] * len(partners),
        scratch_shapes=[pltpu.SemaphoreType.DMA((len(partners), 2))],
        compiler_params=LIMIT,
        name="head_slices",
    )(far(keys), far(values))
    return pieces


def pack_kernel(ids_ref, queries_ref, out_ref):
    owned, steps, _ = queries_ref.shape
    rows = owned * steps * GROUP
    lane = lax.broadcasted_iota(jnp.int32, (out_ref.shape[1] - rows, LANES), 1)
    marks = jnp.zeros(lane.shape, jnp.float32)
    for n in range(owned):
        marks = jnp.where(lane == n, ids_ref[n].astype(jnp.float32), marks)
    marks = marks.astype(jnp.bfloat16)
    for head in range(KEY_VALUE_HEADS):
        parts = []
        for n in range(owned):
            for r in range(GROUP):
                first = (head * GROUP + r) * HEAD_SIZE
                parts.append(queries_ref[n, :, first : first + HEAD_SIZE].astype(jnp.float32))
        block = jnp.concatenate(parts, axis=0).astype(jnp.bfloat16)
        for copy in range(out_ref.shape[0] // KEY_VALUE_HEADS):
            out_ref[copy * KEY_VALUE_HEADS + head, :rows, :] = block
            out_ref[copy * KEY_VALUE_HEADS + head, rows:, :] = marks


def pack_queries(queries, prompt_id, device_count):
    owned, steps, _ = queries.shape
    rows = owned * steps * GROUP
    packed = pl.pallas_call(
        pack_kernel,
        out_shape=jax.ShapeDtypeStruct((device_count, rows + 16, HEAD_SIZE), jnp.bfloat16),
        in_specs=[whole(pltpu.SMEM), whole()],
        out_specs=whole(),
        compiler_params=LIMIT,
        name="pack_queries",
    )(far(prompt_id), far(queries))
    return packed


def contract(left, right, dims):
    return lax.dot_general(left, right, (dims, ((), ())), preferred_element_type=jnp.float32)


def diagonal(rows):
    row = lax.broadcasted_iota(jnp.int32, (rows, LANES), 0)
    lane = lax.broadcasted_iota(jnp.int32, (rows, LANES), 1)
    return (lane == row) | (lane == row + rows)


def diagonal_row(columns, mask):
    return jnp.sum(jnp.where(mask, columns, 0.0), axis=0, keepdims=True)


def max_and_total(peak, total):
    rows = peak.shape[0]
    lane = lax.broadcasted_iota(jnp.int32, (rows, LANES), 1)
    return jnp.where(lane < LANES // 2, peak, total)


def suffix_kernel(len_ref, query_ref, keys_ref, values_ref, new_keys_ref, new_values_ref, out_ref, aux_ref):
    owned, _, _ = keys_ref.shape
    steps = new_keys_ref.shape[1]
    rows = steps * GROUP
    aux_parts = []
    for n in range(owned):
        query = query_ref[0, n * rows : (n + 1) * rows, :]
        cache = contract(query, keys_ref[n], ((1,), (1,))) * SCALING
        fresh = contract(query, new_keys_ref[n], ((1,), (1,))) * SCALING
        cache_live = lax.broadcasted_iota(jnp.int32, cache.shape, 1) < len_ref[n]
        fresh_live = (
            lax.broadcasted_iota(jnp.int32, fresh.shape, 1)
            <= lax.broadcasted_iota(jnp.int32, fresh.shape, 0) % steps
        )
        peak = jnp.maximum(
            jnp.max(jnp.where(cache_live, cache, -jnp.inf), axis=1, keepdims=True),
            jnp.max(jnp.where(fresh_live, fresh, -jnp.inf), axis=1, keepdims=True),
        )
        cache_exp = jnp.where(cache_live, jnp.exp(cache - peak), 0.0)
        fresh_exp = jnp.where(fresh_live, jnp.exp(fresh - peak), 0.0)
        total = jnp.sum(cache_exp, axis=1, keepdims=True) + jnp.sum(fresh_exp, axis=1, keepdims=True)
        out = contract(cache_exp.astype(jnp.bfloat16), values_ref[n], ((1,), (0,))) + contract(
            fresh_exp.astype(jnp.bfloat16), new_values_ref[n], ((1,), (0,))
        )
        out_ref[0, n * rows : (n + 1) * rows, :] = out
        aux_parts.append(max_and_total(peak, total))
    aux_ref[0] = diagonal_row(jnp.concatenate(aux_parts, axis=0), diagonal(owned * rows))


def suffix_part(suffix_len, packed, keys, values, new_keys, new_values):
    owned, slots, _ = keys.shape
    steps = new_keys.shape[1]
    rows = owned * steps * GROUP
    return pl.pallas_call(
        suffix_kernel,
        grid_spec=pltpu.PrefetchScalarGridSpec(
            num_scalar_prefetch=1,
            grid=(KEY_VALUE_HEADS,),
            in_specs=[
                pl.BlockSpec((1, packed.shape[1], HEAD_SIZE), lambda h, _: (h, 0, 0)),
                pl.BlockSpec((owned, slots, HEAD_SIZE), lambda h, _: (0, 0, h)),
                pl.BlockSpec((owned, slots, HEAD_SIZE), lambda h, _: (0, 0, h)),
                pl.BlockSpec((owned, steps, HEAD_SIZE), lambda h, _: (0, 0, h)),
                pl.BlockSpec((owned, steps, HEAD_SIZE), lambda h, _: (0, 0, h)),
            ],
            out_specs=[
                pl.BlockSpec((1, rows, HEAD_SIZE), lambda h, _: (h, 0, 0)),
                pl.BlockSpec((1, 1, LANES), lambda h, _: (h, 0, 0)),
            ],
        ),
        out_shape=[
            jax.ShapeDtypeStruct((KEY_VALUE_HEADS, rows, HEAD_SIZE), jnp.float32),
            jax.ShapeDtypeStruct((KEY_VALUE_HEADS, 1, LANES), jnp.float32),
        ],
        compiler_params=LIMIT,
        name="suffix_part",
    )(suffix_len, packed, keys, values, new_keys, new_values)


def attend(query, pieces, prompt, state):
    for piece in pieces:
        score = contract(query, piece[0, prompt], ((1,), (1,)))
        peak = jnp.max(score, axis=1, keepdims=True)
        weight = jnp.exp2((score - peak) * WEIGHT_SCALE)
        total = jnp.sum(weight, axis=1, keepdims=True)
        part = contract(weight.astype(jnp.bfloat16), piece[1, prompt], ((1,), (0,)))
        peak = jnp.broadcast_to(peak * SCALING, part.shape)
        total = jnp.broadcast_to(total, part.shape)
        if state is None:
            state = (peak, total, part)
        else:
            best, mass, acc = state
            top = jnp.maximum(best, peak)
            old = jnp.exp(best - top)
            new = jnp.exp(peak - top)
            state = (top, mass * old + total * new, acc * old + part * new)
    return state


def find_places(ids_ref, place_ref, count_ref, rows):
    samples = ids_ref.shape[0]
    prompts = count_ref.shape[0]
    per_prompt = samples // prompts
    for p in range(prompts):
        count_ref[p] = 0

    def one(sample, carry):
        prompt = ids_ref[sample]
        rank = count_ref[prompt]
        count_ref[prompt] = rank + 1
        place_ref[sample] = (prompt * per_prompt + rank) * rows
        return carry

    lax.fori_loop(0, samples, one, 0, unroll=8)


def first_kernel(rows, chunk, ids_ref, queries_ref, *refs):
    pieces, refs = refs[:-6], refs[-6:]
    sorted_ref, out_ref, peak_ref, total_ref, place_ref, count_ref = refs
    devices = queries_ref.shape[0]
    owned = ids_ref.shape[0] // devices
    prompts = count_ref.shape[0]
    find_places(ids_ref, place_ref, count_ref, rows)

    def sort_one(device, carry):
        for n in range(owned):
            target = pl.ds(pl.multiple_of(place_ref[device * owned + n], rows), rows)
            sorted_ref[target, :] = queries_ref[device, n * rows : (n + 1) * rows, :]
        return carry

    lax.fori_loop(0, devices, sort_one, 0, unroll=4)
    chunks = sorted_ref.shape[0] // prompts // chunk

    def step(index, carry):
        target = pl.ds(pl.multiple_of(index * chunk, chunk), chunk)
        peak, total, out = attend(sorted_ref[target, :], pieces, index // chunks, None)
        out_ref[target, :] = out
        peak_ref[target, :] = peak
        total_ref[target, :] = total
        return carry

    lax.fori_loop(0, prompts * chunks, step, 0)


def next_kernel(chunk, sorted_ref, acc_in, peak_in, total_in, *refs):
    pieces, (acc_ref, peak_ref, total_ref) = refs[:-3], refs[-3:]
    prompts = pieces[0].shape[1]
    chunks = sorted_ref.shape[0] // prompts // chunk

    def step(index, carry):
        target = pl.ds(pl.multiple_of(index * chunk, chunk), chunk)
        state = (peak_in[target, :], total_in[target, :], acc_in[target, :])
        peak, total, out = attend(sorted_ref[target, :], pieces, index // chunks, state)
        acc_ref[target, :] = out
        peak_ref[target, :] = peak
        total_ref[target, :] = total
        return carry

    lax.fori_loop(0, prompts * chunks, step, 0)


def last_kernel(rows, chunk, ids_ref, sorted_ref, acc_ref, peak_ref, total_ref, *refs):
    pieces, refs = refs[:-5], refs[-5:]
    out_ref, out_scratch, aux_scratch, place_ref, count_ref = refs
    devices = out_ref.shape[0]
    owned = ids_ref.shape[0] // devices
    prompts = count_ref.shape[0]
    find_places(ids_ref, place_ref, count_ref, rows)
    chunks = sorted_ref.shape[0] // prompts // chunk

    def step(index, carry):
        target = pl.ds(pl.multiple_of(index * chunk, chunk), chunk)
        state = (peak_ref[target, :], total_ref[target, :], acc_ref[target, :])
        peak, total, out = attend(sorted_ref[target, :], pieces, index // chunks, state)
        out_scratch[target, :] = out
        aux_scratch[target, :] = max_and_total(peak, total)
        return carry

    lax.fori_loop(0, prompts * chunks, step, 0)

    mask = diagonal(owned * rows)

    def emit(device, carry):
        aux_parts = []
        for n in range(owned):
            source = pl.ds(pl.multiple_of(place_ref[device * owned + n], rows), rows)
            out_ref[device, n * rows : (n + 1) * rows, :] = out_scratch[source, :]
            aux_parts.append(aux_scratch[source, :])
        row = diagonal_row(jnp.concatenate(aux_parts, axis=0), mask)
        out_ref[device, owned * rows :, :] = jnp.broadcast_to(row, (8, LANES))
        return carry

    lax.fori_loop(0, devices, emit, 0, unroll=4)


def first_stage(ids, queries, pieces, rows):
    samples = ids.shape[0]
    prompts = pieces[0].shape[1]
    total = samples * rows
    results = pl.pallas_call(
        functools.partial(first_kernel, rows, min(256, total // prompts)),
        out_shape=[
            jax.ShapeDtypeStruct((total, HEAD_SIZE), jnp.bfloat16),
            jax.ShapeDtypeStruct((total, HEAD_SIZE), jnp.float32),
            jax.ShapeDtypeStruct((total, LANES), jnp.float32),
            jax.ShapeDtypeStruct((total, LANES), jnp.float32),
        ],
        in_specs=[whole(pltpu.SMEM)] + [whole()] * (1 + len(pieces)),
        out_specs=[whole()] * 4,
        scratch_shapes=[pltpu.SMEM((samples,), jnp.int32), pltpu.SMEM((prompts,), jnp.int32)],
        compiler_params=LIMIT,
        name="first_stage",
    )(ids, queries, *pieces)
    return [near(result) for result in results]


def next_stage(state, pieces):
    total = state[0].shape[0]
    prompts = pieces[0].shape[1]
    results = pl.pallas_call(
        functools.partial(next_kernel, min(256, total // prompts)),
        out_shape=[jax.ShapeDtypeStruct((total, HEAD_SIZE), jnp.float32)] * 3,
        in_specs=[whole()] * (4 + len(pieces)),
        out_specs=[whole()] * 3,
        compiler_params=LIMIT,
        name="next_stage",
    )(*state, *pieces)
    return [state[0]] + [near(result) for result in results]


def last_stage(ids, state, pieces, rows, devices):
    samples = ids.shape[0]
    prompts = pieces[0].shape[1]
    total = samples * rows
    return (
        pl.pallas_call(
            functools.partial(last_kernel, rows, min(256, total // prompts)),
            out_shape=jax.ShapeDtypeStruct((devices, total // devices + 8, HEAD_SIZE), jnp.float32),
            in_specs=[whole(pltpu.SMEM)] + [whole()] * (4 + len(pieces)),
            out_specs=whole(),
            scratch_shapes=[
                pltpu.VMEM((total, HEAD_SIZE), jnp.float32),
                pltpu.VMEM((total, HEAD_SIZE), jnp.float32),
                pltpu.SMEM((samples,), jnp.int32),
                pltpu.SMEM((prompts,), jnp.int32),
            ],
            compiler_params=LIMIT,
            name="last_stage",
        )(ids, *state, *pieces)
    )


def merge_kernel(got_ref, local_ref, local_aux_ref, out_ref):
    owned, steps, _ = out_ref.shape
    rows = local_ref.shape[1]
    half = LANES // 2
    groups = got_ref.shape[0] // KEY_VALUE_HEADS
    aux = [local_aux_ref[:, 0, :]]
    for g in range(groups):
        aux.append(
            jnp.concatenate(
                [got_ref[g * KEY_VALUE_HEADS + h, rows : rows + 1, :] for h in range(KEY_VALUE_HEADS)],
                axis=0,
            )
        )
    peaks = [a[:, :half] for a in aux]
    totals = [a[:, half:] for a in aux]
    highest = functools.reduce(jnp.maximum, peaks)
    scales = [jnp.exp(peak - highest) for peak in peaks]
    denominator = functools.reduce(jnp.add, [t * s for t, s in zip(totals, scales)])
    factors = [jnp.transpose(s / denominator) for s in scales]
    for h in range(KEY_VALUE_HEADS):
        result = local_ref[h] * factors[0][:, h : h + 1]
        for g in range(groups):
            result += got_ref[g * KEY_VALUE_HEADS + h, :rows, :] * factors[g + 1][:, h : h + 1]
        for n in range(owned):
            for r in range(GROUP):
                first = (h * GROUP + r) * HEAD_SIZE
                start = (n * GROUP + r) * steps
                out_ref[n, :, first : first + HEAD_SIZE] = result[start : start + steps, :].astype(
                    jnp.bfloat16
                )


def merge(got, local, local_aux, shape):
    return pl.pallas_call(
        merge_kernel,
        out_shape=jax.ShapeDtypeStruct(shape, jnp.bfloat16),
        in_specs=[whole()] * 3,
        out_specs=whole(),
        compiler_params=LIMIT,
        name="merge",
    )(got, local, local_aux)


def body(
    queries,
    step_keys,
    step_values,
    sample_keys,
    sample_values,
    suffix_len,
    prompt_id,
    document_keys,
    document_values,
):
    owned, steps, _ = queries.shape
    devices = lax.axis_size("seq")
    rows = steps * GROUP
    assert 2 * owned * rows == LANES and devices % KEY_VALUE_HEADS == 0
    arrived = {}

    def exchange(piece, partner):
        route = [(i, i ^ partner) for i in range(devices)]
        arrived[partner] = near(lax.ppermute(piece, "seq", route))

    early = head_slices(document_keys, document_values, EARLY)
    for partner, piece in zip(EARLY, early):
        exchange(piece, partner)
    packed = pack_queries(queries, prompt_id, devices)
    head_queries = lax.all_to_all(packed, "seq", split_axis=0, concat_axis=0, tiled=True)
    late = head_slices(document_keys, document_values, LATE + (0,))
    arrived[0] = near(late[-1])
    for partner, piece in zip(LATE, late):
        exchange(piece, partner)
    head_ids = head_queries[:, owned * rows, :owned].reshape(-1).astype(jnp.int32)
    state = first_stage(
        head_ids, near(head_queries), [arrived[k] for k in (0, 6, 7)], rows
    )
    state = next_stage(state, [arrived[k] for k in (1, 4, 2)])
    sent = last_stage(head_ids, state, [arrived[k] for k in (5, 3)], rows, devices)
    local, local_aux = suffix_part(
        suffix_len, packed, far(sample_keys), far(sample_values), step_keys, step_values
    )
    got = near(lax.all_to_all(sent, "seq", split_axis=0, concat_axis=0, tiled=True))
    return merge(got, near(local), near(local_aux), queries.shape)


def solution(mesh):
    shared = P(("groups", "seq"), None, None)
    split = P("groups", "seq", None)
    return jax.shard_map(
        body,
        mesh=mesh,
        in_specs=(shared,) * 5 + (P(("groups", "seq")),) * 2 + (split,) * 2,
        out_specs=shared,
        check_vma=False,
    )
```

```python
import functools
import math

import jax
import jax.numpy as jnp
from jax import lax
from jax.experimental import pallas as pl
from jax.experimental.pallas import tpu as pltpu
from jax.sharding import PartitionSpec as P


QUERY_HEADS = 64
KEY_VALUE_HEADS = 8
HEAD_SIZE = 128
GROUP = QUERY_HEADS // KEY_VALUE_HEADS
SCALING = HEAD_SIZE ** (-0.5)
LANES = 128
EARLY = (6, 7)
LATE = (4, 2, 5, 3, 1)
LIMIT = pltpu.CompilerParams(vmem_limit_bytes=24 * 1024 * 1024)
LEVELS = 32767.0
CODE_STEPS = 256.0
REST_STEPS = 65000.0
TINY = 2.0**-120
AUX_ROWS = 16
WEIGHT_SCALE = SCALING * math.log2(math.e)


def whole(space=pltpu.VMEM):
    return pl.BlockSpec(memory_space=space)


def near(array):
    return pltpu.with_memory_space_constraint(array, pltpu.VMEM)


def far(array):
    return pltpu.with_memory_space_constraint(array, pltpu.HBM)


def slice_kernel(partners, keys_ref, values_ref, *refs):
    out_refs, sem = refs[:-1], refs[-1]
    mine = lax.axis_index("seq") % KEY_VALUE_HEADS
    copies = []
    for slot, partner in enumerate(partners):
        head = jnp.bitwise_xor(mine, partner)
        columns = pl.ds(pl.multiple_of(head * HEAD_SIZE, HEAD_SIZE), HEAD_SIZE)
        for side, source in enumerate((keys_ref, values_ref)):
            copy = pltpu.make_async_copy(
                source.at[:, :, columns], out_refs[slot].at[side], sem.at[slot, side]
            )
            copy.start()
            copies.append(copy)
    for copy in copies:
        copy.wait()


def head_slices(keys, values, partners):
    prompts, block, _ = keys.shape
    piece = jax.ShapeDtypeStruct((2, prompts, block, HEAD_SIZE), keys.dtype)
    pieces = pl.pallas_call(
        functools.partial(slice_kernel, partners),
        out_shape=[piece] * len(partners),
        in_specs=[whole(pltpu.HBM)] * 2,
        out_specs=[whole()] * len(partners),
        scratch_shapes=[pltpu.SemaphoreType.DMA((len(partners), 2))],
        compiler_params=LIMIT,
        name="head_slices",
    )(far(keys), far(values))
    return pieces


def pack_kernel(ids_ref, queries_ref, out_ref):
    owned, steps, _ = queries_ref.shape
    rows = owned * steps * GROUP
    lane = lax.broadcasted_iota(jnp.int32, (out_ref.shape[1] - rows, LANES), 1)
    marks = jnp.zeros(lane.shape, jnp.float32)
    for n in range(owned):
        marks = jnp.where(lane == n, ids_ref[n].astype(jnp.float32), marks)
    marks = marks.astype(jnp.bfloat16)
    for head in range(KEY_VALUE_HEADS):
        parts = []
        for n in range(owned):
            for r in range(GROUP):
                first = (head * GROUP + r) * HEAD_SIZE
                parts.append(queries_ref[n, :, first : first + HEAD_SIZE].astype(jnp.float32))
        block = jnp.concatenate(parts, axis=0).astype(jnp.bfloat16)
        for copy in range(out_ref.shape[0] // KEY_VALUE_HEADS):
            out_ref[copy * KEY_VALUE_HEADS + head, :rows, :] = block
            out_ref[copy * KEY_VALUE_HEADS + head, rows:, :] = marks


def pack_queries(queries, prompt_id, device_count):
    owned, steps, _ = queries.shape
    rows = owned * steps * GROUP
    packed = pl.pallas_call(
        pack_kernel,
        out_shape=jax.ShapeDtypeStruct((device_count, rows + 16, HEAD_SIZE), jnp.bfloat16),
        in_specs=[whole(pltpu.SMEM), whole()],
        out_specs=whole(),
        compiler_params=LIMIT,
        name="pack_queries",
    )(far(prompt_id), far(queries))
    return packed


def contract(left, right, dims):
    return lax.dot_general(left, right, (dims, ((), ())), preferred_element_type=jnp.float32)


def diagonal(rows):
    row = lax.broadcasted_iota(jnp.int32, (rows, LANES), 0)
    lane = lax.broadcasted_iota(jnp.int32, (rows, LANES), 1)
    return (lane == row) | (lane == row + rows)


def diagonal_row(columns, mask):
    return jnp.sum(jnp.where(mask, columns, 0.0), axis=0, keepdims=True)


def left_right(left, right):
    lane = lax.broadcasted_iota(jnp.int32, (left.shape[0], LANES), 1)
    return jnp.where(lane < LANES // 2, left, right)


def to_words(values):
    return jnp.round(values).astype(jnp.int32).astype(jnp.int16)


def from_words(words):
    return words.astype(jnp.int32).astype(jnp.float32)


def suffix_kernel(len_ref, query_ref, keys_ref, values_ref, new_keys_ref, new_values_ref, out_ref, aux_ref):
    owned, _, _ = keys_ref.shape
    steps = new_keys_ref.shape[1]
    rows = steps * GROUP
    aux_parts = []
    for n in range(owned):
        query = query_ref[0, n * rows : (n + 1) * rows, :]
        cache = contract(query, keys_ref[n], ((1,), (1,))) * SCALING
        fresh = contract(query, new_keys_ref[n], ((1,), (1,))) * SCALING
        cache_live = lax.broadcasted_iota(jnp.int32, cache.shape, 1) < len_ref[n]
        fresh_live = (
            lax.broadcasted_iota(jnp.int32, fresh.shape, 1)
            <= lax.broadcasted_iota(jnp.int32, fresh.shape, 0) % steps
        )
        peak = jnp.maximum(
            jnp.max(jnp.where(cache_live, cache, -jnp.inf), axis=1, keepdims=True),
            jnp.max(jnp.where(fresh_live, fresh, -jnp.inf), axis=1, keepdims=True),
        )
        cache_exp = jnp.where(cache_live, jnp.exp(cache - peak), 0.0)
        fresh_exp = jnp.where(fresh_live, jnp.exp(fresh - peak), 0.0)
        total = jnp.sum(cache_exp, axis=1, keepdims=True) + jnp.sum(fresh_exp, axis=1, keepdims=True)
        out = contract(cache_exp.astype(jnp.bfloat16), values_ref[n], ((1,), (0,))) + contract(
            fresh_exp.astype(jnp.bfloat16), new_values_ref[n], ((1,), (0,))
        )
        out_ref[0, n * rows : (n + 1) * rows, :] = out
        aux_parts.append(left_right(peak, total))
    aux_ref[0] = diagonal_row(jnp.concatenate(aux_parts, axis=0), diagonal(owned * rows))


def suffix_part(suffix_len, packed, keys, values, new_keys, new_values):
    owned, slots, _ = keys.shape
    steps = new_keys.shape[1]
    rows = owned * steps * GROUP
    return pl.pallas_call(
        suffix_kernel,
        grid_spec=pltpu.PrefetchScalarGridSpec(
            num_scalar_prefetch=1,
            grid=(KEY_VALUE_HEADS,),
            in_specs=[
                pl.BlockSpec((1, packed.shape[1], HEAD_SIZE), lambda h, _: (h, 0, 0)),
                pl.BlockSpec((owned, slots, HEAD_SIZE), lambda h, _: (0, 0, h)),
                pl.BlockSpec((owned, slots, HEAD_SIZE), lambda h, _: (0, 0, h)),
                pl.BlockSpec((owned, steps, HEAD_SIZE), lambda h, _: (0, 0, h)),
                pl.BlockSpec((owned, steps, HEAD_SIZE), lambda h, _: (0, 0, h)),
            ],
            out_specs=[
                pl.BlockSpec((1, rows, HEAD_SIZE), lambda h, _: (h, 0, 0)),
                pl.BlockSpec((1, 1, LANES), lambda h, _: (h, 0, 0)),
            ],
        ),
        out_shape=[
            jax.ShapeDtypeStruct((KEY_VALUE_HEADS, rows, HEAD_SIZE), jnp.float32),
            jax.ShapeDtypeStruct((KEY_VALUE_HEADS, 1, LANES), jnp.float32),
        ],
        compiler_params=LIMIT,
        name="suffix_part",
    )(suffix_len, packed, keys, values, new_keys, new_values)


def attend(query, pieces, prompt, state):
    for piece in pieces:
        score = contract(query, piece[0, prompt], ((1,), (1,)))
        peak = jnp.max(score, axis=1, keepdims=True)
        weight = jnp.exp2((score - peak) * WEIGHT_SCALE)
        total = jnp.sum(weight, axis=1, keepdims=True)
        part = contract(weight.astype(jnp.bfloat16), piece[1, prompt], ((1,), (0,)))
        peak = jnp.broadcast_to(peak * SCALING, part.shape)
        total = jnp.broadcast_to(total, part.shape)
        if state is None:
            state = (peak, total, part)
        else:
            best, mass, acc = state
            top = jnp.maximum(best, peak)
            old = jnp.exp(best - top)
            new = jnp.exp(peak - top)
            state = (top, mass * old + total * new, acc * old + part * new)
    return state


def find_places(ids, prompts, rows):
    samples = ids.shape[0]
    order = jnp.arange(samples, dtype=jnp.int32)
    earlier = (ids[None, :] == ids[:, None]) & (order[None, :] < order[:, None])
    rank = jnp.sum(earlier.astype(jnp.int32), axis=1)
    return (ids * (samples // prompts) + rank) * rows


def first_kernel(rows, chunk, place_ref, queries_ref, *refs):
    pieces, refs = refs[:-4], refs[-4:]
    sorted_ref, out_ref, peak_ref, total_ref = refs
    devices = queries_ref.shape[0]
    owned = place_ref.shape[0] // devices
    prompts = pieces[0].shape[1]

    def sort_one(device, carry):
        for n in range(owned):
            target = pl.ds(pl.multiple_of(place_ref[device * owned + n], rows), rows)
            sorted_ref[target, :] = queries_ref[device, n * rows : (n + 1) * rows, :]
        return carry

    lax.fori_loop(0, devices, sort_one, 0, unroll=4)
    chunks = sorted_ref.shape[0] // prompts // chunk

    def step(index, carry):
        target = pl.ds(pl.multiple_of(index * chunk, chunk), chunk)
        peak, total, out = attend(sorted_ref[target, :], pieces, index // chunks, None)
        out_ref[target, :] = out
        peak_ref[target, :] = peak
        total_ref[target, :] = total
        return carry

    lax.fori_loop(0, prompts * chunks, step, 0)


def next_kernel(chunk, sorted_ref, acc_in, peak_in, total_in, *refs):
    pieces, (acc_ref, peak_ref, total_ref) = refs[:-3], refs[-3:]
    prompts = pieces[0].shape[1]
    chunks = sorted_ref.shape[0] // prompts // chunk

    def step(index, carry):
        target = pl.ds(pl.multiple_of(index * chunk, chunk), chunk)
        state = (peak_in[target, :], total_in[target, :], acc_in[target, :])
        peak, total, out = attend(sorted_ref[target, :], pieces, index // chunks, state)
        acc_ref[target, :] = out
        peak_ref[target, :] = peak
        total_ref[target, :] = total
        return carry

    lax.fori_loop(0, prompts * chunks, step, 0)


def last_kernel(rows, chunk, place_ref, sorted_ref, acc_ref, peak_ref, total_ref, *refs):
    pieces, refs = refs[:-3], refs[-3:]
    out_ref, out_scratch, aux_scratch = refs
    devices = out_ref.shape[0]
    owned = place_ref.shape[0] // devices
    prompts = pieces[0].shape[1]
    chunks = sorted_ref.shape[0] // prompts // chunk

    def step(index, carry):
        target = pl.ds(pl.multiple_of(index * chunk, chunk), chunk)
        state = (peak_ref[target, :], total_ref[target, :], acc_ref[target, :])
        peak, total, out = attend(sorted_ref[target, :], pieces, index // chunks, state)
        out = out / total
        largest = jnp.max(jnp.abs(out), axis=1, keepdims=True)
        code = jnp.ceil(jnp.log2(jnp.maximum(largest, TINY)) * CODE_STEPS)
        out = out * (LEVELS * jnp.exp2(code * (-1.0 / CODE_STEPS)))
        out_scratch[target, :] = to_words(jnp.clip(out, -LEVELS, LEVELS))
        aux_scratch[target, :] = left_right(peak + jnp.log(total), code)
        return carry

    lax.fori_loop(0, prompts * chunks, step, 0)

    mask = diagonal(owned * rows)
    first_rows = lax.broadcasted_iota(jnp.int32, (AUX_ROWS, LANES), 0) < AUX_ROWS // 2

    def emit(device, carry):
        aux_parts = []
        for n in range(owned):
            source = pl.ds(pl.multiple_of(place_ref[device * owned + n], rows), rows)
            out_ref[device, n * rows : (n + 1) * rows, :] = out_scratch[source, :]
            aux_parts.append(aux_scratch[source, :])
        row = diagonal_row(jnp.concatenate(aux_parts, axis=0), mask)
        near_part = jnp.round(row)
        rest = (row - near_part) * REST_STEPS
        words = jnp.where(first_rows, near_part, rest)
        out_ref[device, owned * rows :, :] = to_words(words)
        return carry

    lax.fori_loop(0, devices, emit, 0, unroll=4)


def first_stage(places, queries, pieces, rows):
    prompts = pieces[0].shape[1]
    total = places.shape[0] * rows
    results = pl.pallas_call(
        functools.partial(first_kernel, rows, min(256, total // prompts)),
        out_shape=[
            jax.ShapeDtypeStruct((total, HEAD_SIZE), jnp.bfloat16),
            jax.ShapeDtypeStruct((total, HEAD_SIZE), jnp.float32),
            jax.ShapeDtypeStruct((total, LANES), jnp.float32),
            jax.ShapeDtypeStruct((total, LANES), jnp.float32),
        ],
        in_specs=[whole(pltpu.SMEM)] + [whole()] * (1 + len(pieces)),
        out_specs=[whole()] * 4,
        compiler_params=LIMIT,
        name="first_stage",
    )(places, queries, *pieces)
    return [near(result) for result in results]


def next_stage(state, pieces):
    total = state[0].shape[0]
    prompts = pieces[0].shape[1]
    results = pl.pallas_call(
        functools.partial(next_kernel, min(256, total // prompts)),
        out_shape=[jax.ShapeDtypeStruct((total, HEAD_SIZE), jnp.float32)] * 3,
        in_specs=[whole()] * (4 + len(pieces)),
        out_specs=[whole()] * 3,
        compiler_params=LIMIT,
        name="next_stage",
    )(*state, *pieces)
    return [state[0]] + [near(result) for result in results]


def last_stage(places, state, pieces, rows, devices):
    prompts = pieces[0].shape[1]
    total = places.shape[0] * rows
    return pl.pallas_call(
        functools.partial(last_kernel, rows, min(256, total // prompts)),
        out_shape=jax.ShapeDtypeStruct((devices, total // devices + AUX_ROWS, HEAD_SIZE), jnp.int16),
        in_specs=[whole(pltpu.SMEM)] + [whole()] * (4 + len(pieces)),
        out_specs=whole(),
        scratch_shapes=[
            pltpu.VMEM((total, HEAD_SIZE), jnp.int16),
            pltpu.VMEM((total, HEAD_SIZE), jnp.float32),
        ],
        compiler_params=LIMIT,
        name="last_stage",
    )(places, *state, *pieces)


def merge_kernel(got_ref, local_ref, local_aux_ref, out_ref):
    owned, steps, _ = out_ref.shape
    rows = local_ref.shape[1]
    half = LANES // 2
    groups = got_ref.shape[0] // KEY_VALUE_HEADS
    local_aux = local_aux_ref[:, 0, :]
    local_total = local_aux[:, half:]
    levels = [local_aux[:, :half] + jnp.log(local_total)]
    scales = [1.0 / local_total]
    for g in range(groups):
        both = []
        for h in range(KEY_VALUE_HEADS):
            words = from_words(got_ref[g * KEY_VALUE_HEADS + h, rows:, :])
            middle = AUX_ROWS // 2
            both.append(words[:1] + words[middle : middle + 1] * (1.0 / REST_STEPS))
        aux = jnp.concatenate(both, axis=0)
        levels.append(aux[:, :half])
        scales.append(jnp.exp2(aux[:, half:] * (1.0 / CODE_STEPS)) * (1.0 / LEVELS))
    highest = functools.reduce(jnp.maximum, levels)
    weights = [jnp.exp(level - highest) for level in levels]
    denominator = functools.reduce(jnp.add, weights)
    factors = [jnp.transpose(w * s / denominator) for w, s in zip(weights, scales)]
    for h in range(KEY_VALUE_HEADS):
        result = local_ref[h] * factors[0][:, h : h + 1]
        for g in range(groups):
            part = from_words(got_ref[g * KEY_VALUE_HEADS + h, :rows, :])
            result += part * factors[g + 1][:, h : h + 1]
        for n in range(owned):
            for r in range(GROUP):
                first = (h * GROUP + r) * HEAD_SIZE
                start = (n * GROUP + r) * steps
                out_ref[n, :, first : first + HEAD_SIZE] = result[start : start + steps, :].astype(
                    jnp.bfloat16
                )


def merge(got, local, local_aux, shape):
    return pl.pallas_call(
        merge_kernel,
        out_shape=jax.ShapeDtypeStruct(shape, jnp.bfloat16),
        in_specs=[whole()] * 3,
        out_specs=whole(),
        compiler_params=LIMIT,
        name="merge",
    )(got, local, local_aux)


def body(
    queries,
    step_keys,
    step_values,
    sample_keys,
    sample_values,
    suffix_len,
    prompt_id,
    document_keys,
    document_values,
):
    owned, steps, _ = queries.shape
    devices = lax.axis_size("seq")
    rows = steps * GROUP
    assert 2 * owned * rows == LANES and devices % KEY_VALUE_HEADS == 0
    arrived = {}

    def exchange(piece, partner):
        route = [(i, i ^ partner) for i in range(devices)]
        arrived[partner] = near(lax.ppermute(piece, "seq", route))

    slices = head_slices(document_keys, document_values, EARLY + LATE + (0,))
    for partner, piece in zip(EARLY, slices):
        exchange(piece, partner)
    packed = pack_queries(queries, prompt_id, devices)
    head_queries = lax.all_to_all(packed, "seq", split_axis=0, concat_axis=0, tiled=True)
    arrived[0] = near(slices[-1])
    for partner, piece in zip(LATE, slices[len(EARLY) :]):
        exchange(piece, partner)
    head_ids = head_queries[:, owned * rows, :owned].reshape(-1).astype(jnp.int32)
    places = find_places(head_ids, document_keys.shape[0], rows)
    state = first_stage(places, near(head_queries), [arrived[k] for k in (0, 6, 7)], rows)
    state = next_stage(state, [arrived[k] for k in (1, 4, 2)])
    sent = last_stage(places, state, [arrived[k] for k in (5, 3)], rows, devices)
    local, local_aux = suffix_part(
        suffix_len, packed, far(sample_keys), far(sample_values), step_keys, step_values
    )
    got = near(lax.all_to_all(sent, "seq", split_axis=0, concat_axis=0, tiled=True))
    return merge(got, near(local), near(local_aux), queries.shape)


def solution(mesh):
    shared = P(("groups", "seq"), None, None)
    split = P("groups", "seq", None)
    return jax.shard_map(
        body,
        mesh=mesh,
        in_specs=(shared,) * 5 + (P(("groups", "seq")),) * 2 + (split,) * 2,
        out_specs=shared,
        check_vma=False,
    )
```

```python
import functools
import math

import jax
import jax.numpy as jnp
from jax import lax
from jax.experimental import pallas as pl
from jax.experimental.pallas import tpu as pltpu
from jax.sharding import PartitionSpec as P


QUERY_HEADS = 64
KEY_VALUE_HEADS = 8
HEAD_SIZE = 128
GROUP = QUERY_HEADS // KEY_VALUE_HEADS
SCALING = HEAD_SIZE ** (-0.5)
LANES = 128
FIRST = (6,)
EARLY = (7, 4)
LATE = (5, 2, 3, 1)
LIMIT = pltpu.CompilerParams(vmem_limit_bytes=24 * 1024 * 1024)
LEVELS = 32767.0
CODE_STEPS = 256.0
REST_STEPS = 65000.0
TINY = 2.0**-120
AUX_ROWS = 8
WEIGHT_SCALE = SCALING * math.log2(math.e)


def whole(space=pltpu.VMEM):
    return pl.BlockSpec(memory_space=space)


def near(array):
    return pltpu.with_memory_space_constraint(array, pltpu.VMEM)


def far(array):
    return pltpu.with_memory_space_constraint(array, pltpu.HBM)


def start_slices(partners, keys_ref, values_ref, out_refs, sem):
    mine = lax.axis_index("seq") % KEY_VALUE_HEADS
    copies = []
    for slot, partner in enumerate(partners):
        head = jnp.bitwise_xor(mine, partner)
        columns = pl.ds(pl.multiple_of(head * HEAD_SIZE, HEAD_SIZE), HEAD_SIZE)
        for side, source in enumerate((keys_ref, values_ref)):
            copy = pltpu.make_async_copy(
                source.at[:, :, columns], out_refs[slot].at[side], sem.at[slot, side]
            )
            copy.start()
            copies.append(copy)
    return copies


def slice_kernel(partners, keys_ref, values_ref, *refs):
    for copy in start_slices(partners, keys_ref, values_ref, refs[:-1], refs[-1]):
        copy.wait()


def head_slices(keys, values, partners):
    prompts, block, _ = keys.shape
    piece = jax.ShapeDtypeStruct((2, prompts, block, HEAD_SIZE), keys.dtype)
    pieces = pl.pallas_call(
        functools.partial(slice_kernel, partners),
        out_shape=[piece] * len(partners),
        in_specs=[whole(pltpu.HBM)] * 2,
        out_specs=[whole()] * len(partners),
        scratch_shapes=[pltpu.SemaphoreType.DMA((len(partners), 2))],
        compiler_params=LIMIT,
        name="head_slices",
    )(far(keys), far(values))
    return pieces


def pack_rows(ids_ref, queries_ref, out_ref):
    owned, steps, _ = queries_ref.shape
    rows = owned * steps * GROUP
    lane = lax.broadcasted_iota(jnp.int32, (out_ref.shape[1] - rows, LANES), 1)
    marks = jnp.zeros(lane.shape, jnp.float32)
    for n in range(owned):
        marks = jnp.where(lane == n, ids_ref[n].astype(jnp.float32), marks)
    marks = marks.astype(jnp.bfloat16)
    for head in range(KEY_VALUE_HEADS):
        parts = []
        for n in range(owned):
            for r in range(GROUP):
                first = (head * GROUP + r) * HEAD_SIZE
                parts.append(queries_ref[n, :, first : first + HEAD_SIZE].astype(jnp.float32))
        block = jnp.concatenate(parts, axis=0).astype(jnp.bfloat16)
        for copy in range(out_ref.shape[0] // KEY_VALUE_HEADS):
            out_ref[copy * KEY_VALUE_HEADS + head, :rows, :] = block
            out_ref[copy * KEY_VALUE_HEADS + head, rows:, :] = marks


def slice_and_pack_kernel(partners, keys_ref, values_ref, ids_ref, queries_ref, *refs):
    out_refs, packed_ref, query_buffer, sem, query_sem = refs[:-4], *refs[-4:]
    load = pltpu.make_async_copy(queries_ref, query_buffer, query_sem)
    load.start()
    copies = start_slices(partners, keys_ref, values_ref, out_refs, sem)
    load.wait()
    pack_rows(ids_ref, query_buffer, packed_ref)
    for copy in copies:
        copy.wait()


def slices_and_queries(keys, values, partners, queries, prompt_id, devices):
    prompts, block, _ = keys.shape
    owned, steps, _ = queries.shape
    piece = jax.ShapeDtypeStruct((2, prompts, block, HEAD_SIZE), keys.dtype)
    rows = owned * steps * GROUP + AUX_ROWS
    results = pl.pallas_call(
        functools.partial(slice_and_pack_kernel, partners),
        out_shape=[piece] * len(partners)
        + [jax.ShapeDtypeStruct((devices, rows, HEAD_SIZE), jnp.bfloat16)],
        in_specs=[whole(pltpu.HBM)] * 2 + [whole(pltpu.SMEM), whole(pltpu.HBM)],
        out_specs=[whole()] * (len(partners) + 1),
        scratch_shapes=[
            pltpu.VMEM(queries.shape, queries.dtype),
            pltpu.SemaphoreType.DMA((len(partners), 2)),
            pltpu.SemaphoreType.DMA,
        ],
        compiler_params=LIMIT,
        name="slices_and_queries",
    )(far(keys), far(values), far(prompt_id), far(queries))
    return results[:-1], results[-1]


def contract(left, right, dims):
    return lax.dot_general(left, right, (dims, ((), ())), preferred_element_type=jnp.float32)


def diagonal(rows):
    row = lax.broadcasted_iota(jnp.int32, (rows, LANES), 0)
    lane = lax.broadcasted_iota(jnp.int32, (rows, LANES), 1)
    return (lane == row) | (lane == row + rows)


def diagonal_row(columns, mask):
    return jnp.sum(jnp.where(mask, columns, 0.0), axis=0, keepdims=True)


def left_right(left, right):
    lane = lax.broadcasted_iota(jnp.int32, (left.shape[0], LANES), 1)
    return jnp.where(lane < LANES // 2, left, right)


def to_words(values):
    return jnp.round(values).astype(jnp.int32).astype(jnp.int16)


def from_words(words):
    return words.astype(jnp.int32).astype(jnp.float32)


def suffix_kernel(len_ref, query_ref, keys_ref, values_ref, new_keys_ref, new_values_ref, out_ref, aux_ref):
    owned, _, _ = keys_ref.shape
    steps = new_keys_ref.shape[1]
    rows = steps * GROUP
    aux_parts = []
    for n in range(owned):
        query = query_ref[0, n * rows : (n + 1) * rows, :]
        cache = contract(query, keys_ref[n], ((1,), (1,))) * SCALING
        fresh = contract(query, new_keys_ref[n], ((1,), (1,))) * SCALING
        cache_live = lax.broadcasted_iota(jnp.int32, cache.shape, 1) < len_ref[n]
        fresh_live = (
            lax.broadcasted_iota(jnp.int32, fresh.shape, 1)
            <= lax.broadcasted_iota(jnp.int32, fresh.shape, 0) % steps
        )
        peak = jnp.maximum(
            jnp.max(jnp.where(cache_live, cache, -jnp.inf), axis=1, keepdims=True),
            jnp.max(jnp.where(fresh_live, fresh, -jnp.inf), axis=1, keepdims=True),
        )
        cache_exp = jnp.where(cache_live, jnp.exp(cache - peak), 0.0)
        fresh_exp = jnp.where(fresh_live, jnp.exp(fresh - peak), 0.0)
        total = jnp.sum(cache_exp, axis=1, keepdims=True) + jnp.sum(fresh_exp, axis=1, keepdims=True)
        out = contract(cache_exp.astype(jnp.bfloat16), values_ref[n], ((1,), (0,))) + contract(
            fresh_exp.astype(jnp.bfloat16), new_values_ref[n], ((1,), (0,))
        )
        out_ref[0, n * rows : (n + 1) * rows, :] = out
        aux_parts.append(left_right(peak, total))
    aux_ref[0] = diagonal_row(jnp.concatenate(aux_parts, axis=0), diagonal(owned * rows))


def suffix_part(suffix_len, packed, keys, values, new_keys, new_values):
    owned, slots, _ = keys.shape
    steps = new_keys.shape[1]
    rows = owned * steps * GROUP
    return pl.pallas_call(
        suffix_kernel,
        grid_spec=pltpu.PrefetchScalarGridSpec(
            num_scalar_prefetch=1,
            grid=(KEY_VALUE_HEADS,),
            in_specs=[
                pl.BlockSpec((1, packed.shape[1], HEAD_SIZE), lambda h, _: (h, 0, 0)),
                pl.BlockSpec((owned, slots, HEAD_SIZE), lambda h, _: (0, 0, h)),
                pl.BlockSpec((owned, slots, HEAD_SIZE), lambda h, _: (0, 0, h)),
                pl.BlockSpec((owned, steps, HEAD_SIZE), lambda h, _: (0, 0, h)),
                pl.BlockSpec((owned, steps, HEAD_SIZE), lambda h, _: (0, 0, h)),
            ],
            out_specs=[
                pl.BlockSpec((1, rows, HEAD_SIZE), lambda h, _: (h, 0, 0)),
                pl.BlockSpec((1, 1, LANES), lambda h, _: (h, 0, 0)),
            ],
        ),
        out_shape=[
            jax.ShapeDtypeStruct((KEY_VALUE_HEADS, rows, HEAD_SIZE), jnp.float32),
            jax.ShapeDtypeStruct((KEY_VALUE_HEADS, 1, LANES), jnp.float32),
        ],
        compiler_params=LIMIT,
        name="suffix_part",
    )(suffix_len, packed, keys, values, new_keys, new_values)


def attend(query, pieces, prompt, state):
    scores = [contract(query, piece[0, prompt], ((1,), (1,))) for piece in pieces]
    peaks = [jnp.max(score, axis=1, keepdims=True) for score in scores]
    weights = [jnp.exp2((score - peak) * WEIGHT_SCALE) for score, peak in zip(scores, peaks)]
    parts = [
        contract(weight.astype(jnp.bfloat16), piece[1, prompt], ((1,), (0,)))
        for weight, piece in zip(weights, pieces)
    ]
    totals = [jnp.sum(weight, axis=1, keepdims=True) for weight in weights]
    shape = parts[0].shape
    tops = [jnp.broadcast_to(peak * SCALING, shape) for peak in peaks]
    masses = [jnp.broadcast_to(total, shape) for total in totals]
    if state is not None:
        tops.append(state[0])
        masses.append(state[1])
        parts.append(state[2])
    top = functools.reduce(jnp.maximum, tops)
    factors = [jnp.exp(t - top) for t in tops]
    mass = functools.reduce(jnp.add, [m * f for m, f in zip(masses, factors)])
    out = functools.reduce(jnp.add, [p * f for p, f in zip(parts, factors)])
    return top, mass, out


def find_places(ids, prompts, rows):
    samples = ids.shape[0]
    order = jnp.arange(samples, dtype=jnp.int32)
    earlier = (ids[None, :] == ids[:, None]) & (order[None, :] < order[:, None])
    rank = jnp.sum(earlier.astype(jnp.int32), axis=1)
    return (ids * (samples // prompts) + rank) * rows


def first_kernel(rows, chunk, place_ref, queries_ref, *refs):
    pieces, refs = refs[:-4], refs[-4:]
    sorted_ref, out_ref, peak_ref, total_ref = refs
    devices = queries_ref.shape[0]
    owned = place_ref.shape[0] // devices
    prompts = pieces[0].shape[1]

    def sort_one(device, carry):
        for n in range(owned):
            target = pl.ds(pl.multiple_of(place_ref[device * owned + n], rows), rows)
            sorted_ref[target, :] = queries_ref[device, n * rows : (n + 1) * rows, :]
        return carry

    lax.fori_loop(0, devices, sort_one, 0, unroll=4)
    chunks = sorted_ref.shape[0] // prompts // chunk

    def step(index, carry):
        target = pl.ds(pl.multiple_of(index * chunk, chunk), chunk)
        peak, total, out = attend(sorted_ref[target, :], pieces, index // chunks, None)
        out_ref[target, :] = out
        peak_ref[target, :] = peak
        total_ref[target, :] = total
        return carry

    lax.fori_loop(0, prompts * chunks, step, 0, unroll=2)


def last_kernel(rows, chunk, place_ref, sorted_ref, acc_ref, peak_ref, total_ref, *refs):
    pieces, refs = refs[:-3], refs[-3:]
    out_ref, out_scratch, aux_scratch = refs
    devices = out_ref.shape[0]
    owned = place_ref.shape[0] // devices
    prompts = pieces[0].shape[1]
    chunks = sorted_ref.shape[0] // prompts // chunk

    def step(index, carry):
        target = pl.ds(pl.multiple_of(index * chunk, chunk), chunk)
        state = (peak_ref[target, :], total_ref[target, :], acc_ref[target, :])
        peak, total, out = attend(sorted_ref[target, :], pieces, index // chunks, state)
        out = out / total
        largest = jnp.max(jnp.abs(out), axis=1, keepdims=True)
        code = jnp.ceil(jnp.log2(jnp.maximum(largest, TINY)) * CODE_STEPS)
        out = out * (LEVELS * jnp.exp2(code * (-1.0 / CODE_STEPS)))
        out_scratch[target, :] = to_words(jnp.clip(out, -LEVELS, LEVELS))
        aux_scratch[target, :] = left_right(peak + jnp.log(total), code)
        return carry

    lax.fori_loop(0, prompts * chunks, step, 0, unroll=2)

    mask = diagonal(owned * rows)
    first_rows = lax.broadcasted_iota(jnp.int32, (AUX_ROWS, LANES), 0) < AUX_ROWS // 2

    def emit(device, carry):
        aux_parts = []
        for n in range(owned):
            source = pl.ds(pl.multiple_of(place_ref[device * owned + n], rows), rows)
            out_ref[device, n * rows : (n + 1) * rows, :] = out_scratch[source, :]
            aux_parts.append(aux_scratch[source, :])
        row = diagonal_row(jnp.concatenate(aux_parts, axis=0), mask)
        near_part = jnp.round(row)
        rest = (row - near_part) * REST_STEPS
        words = jnp.where(first_rows, near_part, rest)
        out_ref[device, owned * rows :, :] = to_words(words)
        return carry

    lax.fori_loop(0, devices, emit, 0, unroll=4)


def first_stage(places, queries, pieces, rows):
    prompts = pieces[0].shape[1]
    total = places.shape[0] * rows
    results = pl.pallas_call(
        functools.partial(first_kernel, rows, min(512, total // prompts)),
        out_shape=[
            jax.ShapeDtypeStruct((total, HEAD_SIZE), jnp.bfloat16),
            jax.ShapeDtypeStruct((total, HEAD_SIZE), jnp.float32),
            jax.ShapeDtypeStruct((total, LANES), jnp.float32),
            jax.ShapeDtypeStruct((total, LANES), jnp.float32),
        ],
        in_specs=[whole(pltpu.SMEM)] + [whole()] * (1 + len(pieces)),
        out_specs=[whole()] * 4,
        compiler_params=LIMIT,
        name="first_stage",
    )(places, queries, *pieces)
    return [near(result) for result in results]


def last_stage(places, state, pieces, rows, devices):
    prompts = pieces[0].shape[1]
    total = places.shape[0] * rows
    return pl.pallas_call(
        functools.partial(last_kernel, rows, min(512, total // prompts)),
        out_shape=jax.ShapeDtypeStruct((devices, total // devices + AUX_ROWS, HEAD_SIZE), jnp.int16),
        in_specs=[whole(pltpu.SMEM)] + [whole()] * (4 + len(pieces)),
        out_specs=whole(),
        scratch_shapes=[
            pltpu.VMEM((total, HEAD_SIZE), jnp.int16),
            pltpu.VMEM((total, HEAD_SIZE), jnp.float32),
        ],
        compiler_params=LIMIT,
        name="last_stage",
    )(places, *state, *pieces)


def merge_kernel(got_ref, local_ref, local_aux_ref, out_ref):
    owned, steps, _ = out_ref.shape
    rows = local_ref.shape[1]
    half = LANES // 2
    groups = got_ref.shape[0] // KEY_VALUE_HEADS
    local_aux = local_aux_ref[:, 0, :]
    local_total = local_aux[:, half:]
    levels = [local_aux[:, :half] + jnp.log(local_total)]
    scales = [1.0 / local_total]
    for g in range(groups):
        both = []
        for h in range(KEY_VALUE_HEADS):
            words = from_words(got_ref[g * KEY_VALUE_HEADS + h, rows:, :])
            middle = AUX_ROWS // 2
            both.append(words[:1] + words[middle : middle + 1] * (1.0 / REST_STEPS))
        aux = jnp.concatenate(both, axis=0)
        levels.append(aux[:, :half])
        scales.append(jnp.exp2(aux[:, half:] * (1.0 / CODE_STEPS)) * (1.0 / LEVELS))
    highest = functools.reduce(jnp.maximum, levels)
    weights = [jnp.exp(level - highest) for level in levels]
    denominator = functools.reduce(jnp.add, weights)
    factors = [jnp.transpose(w * s / denominator) for w, s in zip(weights, scales)]
    for h in range(KEY_VALUE_HEADS):
        result = local_ref[h] * factors[0][:, h : h + 1]
        for g in range(groups):
            part = from_words(got_ref[g * KEY_VALUE_HEADS + h, :rows, :])
            result += part * factors[g + 1][:, h : h + 1]
        for n in range(owned):
            for r in range(GROUP):
                first = (h * GROUP + r) * HEAD_SIZE
                start = (n * GROUP + r) * steps
                out_ref[n, :, first : first + HEAD_SIZE] = result[start : start + steps, :].astype(
                    jnp.bfloat16
                )


def merge(got, local, local_aux, shape):
    return pl.pallas_call(
        merge_kernel,
        out_shape=jax.ShapeDtypeStruct(shape, jnp.bfloat16),
        in_specs=[whole()] * 3,
        out_specs=whole(),
        compiler_params=LIMIT,
        name="merge",
    )(got, local, local_aux)


def body(
    queries,
    step_keys,
    step_values,
    sample_keys,
    sample_values,
    suffix_len,
    prompt_id,
    document_keys,
    document_values,
):
    owned, steps, _ = queries.shape
    devices = lax.axis_size("seq")
    rows = steps * GROUP
    assert 2 * owned * rows == LANES and devices % KEY_VALUE_HEADS == 0
    arrived = {}

    def exchange(piece, partner):
        route = [(i, i ^ partner) for i in range(devices)]
        arrived[partner] = near(lax.ppermute(piece, "seq", route))

    slices = head_slices(document_keys, document_values, FIRST)
    exchange(slices[0], FIRST[0])
    slices, packed = slices_and_queries(
        document_keys, document_values, EARLY + LATE + (0,), queries, prompt_id, devices
    )
    for partner, piece in zip(EARLY, slices):
        exchange(piece, partner)
    head_queries = lax.all_to_all(packed, "seq", split_axis=0, concat_axis=0, tiled=True)
    arrived[0] = near(slices[-1])
    for partner, piece in zip(LATE, slices[len(EARLY) :]):
        exchange(piece, partner)
    head_ids = head_queries[:, owned * rows, :owned].reshape(-1).astype(jnp.int32)
    places = find_places(head_ids, document_keys.shape[0], rows)
    ready = [arrived[k] for k in (0, 6, 7, 1, 4, 2)]
    state = first_stage(places, near(head_queries), ready, rows)
    sent = last_stage(places, state, [arrived[k] for k in (5, 3)], rows, devices)
    local, local_aux = suffix_part(
        suffix_len, packed, far(sample_keys), far(sample_values), step_keys, step_values
    )
    got = near(lax.all_to_all(sent, "seq", split_axis=0, concat_axis=0, tiled=True))
    return merge(got, near(local), near(local_aux), queries.shape)


def solution(mesh):
    shared = P(("groups", "seq"), None, None)
    split = P("groups", "seq", None)
    return jax.shard_map(
        body,
        mesh=mesh,
        in_specs=(shared,) * 5 + (P(("groups", "seq")),) * 2 + (split,) * 2,
        out_specs=shared,
        check_vma=False,
    )
```

```python
import functools
import math

import jax
import jax.numpy as jnp
from jax import lax
from jax.experimental import pallas as pl
from jax.experimental.pallas import tpu as pltpu
from jax.sharding import PartitionSpec as P


QUERY_HEADS = 64
KEY_VALUE_HEADS = 8
HEAD_SIZE = 128
GROUP = QUERY_HEADS // KEY_VALUE_HEADS
SCALING = HEAD_SIZE ** (-0.5)
LANES = 128
FIRST = (6,)
EARLY = (7, 2)
LATE = (4, 5, 3, 1)
LIMIT = pltpu.CompilerParams(vmem_limit_bytes=24 * 1024 * 1024)
LEVELS = 32767.0
CODE_STEPS = 256.0
REST_STEPS = 65000.0
TINY = 2.0**-100
AUX_ROWS = 8
LOAD_PARTS = 4
WEIGHT_SCALE = SCALING * math.log2(math.e)


def whole(space=pltpu.VMEM):
    return pl.BlockSpec(memory_space=space)


def near(array):
    return pltpu.with_memory_space_constraint(array, pltpu.VMEM)


def far(array):
    return pltpu.with_memory_space_constraint(array, pltpu.HBM)


def start_slices(partners, keys_ref, values_ref, out_refs, sem):
    mine = lax.axis_index("seq") % KEY_VALUE_HEADS
    copies = []
    for slot, partner in enumerate(partners):
        head = jnp.bitwise_xor(mine, partner)
        columns = pl.ds(pl.multiple_of(head * HEAD_SIZE, HEAD_SIZE), HEAD_SIZE)
        for side, source in enumerate((keys_ref, values_ref)):
            copy = pltpu.make_async_copy(
                source.at[:, :, columns], out_refs[slot].at[side], sem.at[slot, side]
            )
            copy.start()
            copies.append(copy)
    return copies


def slice_kernel(partners, keys_ref, values_ref, *refs):
    for copy in start_slices(partners, keys_ref, values_ref, refs[:-1], refs[-1]):
        copy.wait()


def head_slices(keys, values, partners):
    prompts, block, _ = keys.shape
    piece = jax.ShapeDtypeStruct((2, prompts, block, HEAD_SIZE), keys.dtype)
    pieces = pl.pallas_call(
        functools.partial(slice_kernel, partners),
        out_shape=[piece] * len(partners),
        in_specs=[whole(pltpu.HBM)] * 2,
        out_specs=[whole()] * len(partners),
        scratch_shapes=[pltpu.SemaphoreType.DMA((len(partners), 2))],
        compiler_params=LIMIT,
        name="head_slices",
    )(far(keys), far(values))
    return pieces


def pack_rows(ids_ref, queries_ref, out_ref):
    owned, steps, _ = queries_ref.shape
    rows = owned * steps * GROUP
    lane = lax.broadcasted_iota(jnp.int32, (out_ref.shape[1] - rows, LANES), 1)
    marks = jnp.zeros(lane.shape, jnp.float32)
    for n in range(owned):
        marks = jnp.where(lane == n, ids_ref[n].astype(jnp.float32), marks)
    marks = marks.astype(jnp.bfloat16)
    for head in range(KEY_VALUE_HEADS):
        parts = []
        for n in range(owned):
            for r in range(GROUP):
                first = (head * GROUP + r) * HEAD_SIZE
                parts.append(queries_ref[n, :, first : first + HEAD_SIZE].astype(jnp.float32))
        block = jnp.concatenate(parts, axis=0).astype(jnp.bfloat16)
        for copy in range(out_ref.shape[0] // KEY_VALUE_HEADS):
            out_ref[copy * KEY_VALUE_HEADS + head, :rows, :] = block
            out_ref[copy * KEY_VALUE_HEADS + head, rows:, :] = marks


def slice_and_pack_kernel(partners, keys_ref, values_ref, ids_ref, queries_ref, *refs):
    out_refs, packed_ref, query_buffer, sem, query_sem = refs[:-4], *refs[-4:]
    load = pltpu.make_async_copy(queries_ref, query_buffer, query_sem)
    load.start()
    copies = start_slices(partners, keys_ref, values_ref, out_refs, sem)
    load.wait()
    pack_rows(ids_ref, query_buffer, packed_ref)
    for copy in copies:
        copy.wait()


def slices_and_queries(keys, values, partners, queries, prompt_id, devices):
    prompts, block, _ = keys.shape
    owned, steps, _ = queries.shape
    piece = jax.ShapeDtypeStruct((2, prompts, block, HEAD_SIZE), keys.dtype)
    rows = owned * steps * GROUP + AUX_ROWS
    results = pl.pallas_call(
        functools.partial(slice_and_pack_kernel, partners),
        out_shape=[piece] * len(partners)
        + [jax.ShapeDtypeStruct((devices, rows, HEAD_SIZE), jnp.bfloat16)],
        in_specs=[whole(pltpu.HBM)] * 2 + [whole(pltpu.SMEM), whole(pltpu.HBM)],
        out_specs=[whole()] * (len(partners) + 1),
        scratch_shapes=[
            pltpu.VMEM(queries.shape, queries.dtype),
            pltpu.SemaphoreType.DMA((len(partners), 2)),
            pltpu.SemaphoreType.DMA,
        ],
        compiler_params=LIMIT,
        name="slices_and_queries",
    )(far(keys), far(values), far(prompt_id), far(queries))
    return results[:-1], results[-1]


def contract(left, right, dims):
    return lax.dot_general(left, right, (dims, ((), ())), preferred_element_type=jnp.float32)


def diagonal(rows, shift=0):
    row = lax.broadcasted_iota(jnp.int32, (rows, LANES), 0) + shift
    lane = lax.broadcasted_iota(jnp.int32, (rows, LANES), 1)
    return (lane == row) | (lane == row + LANES // 2)


def diagonal_row(columns, mask):
    return jnp.sum(jnp.where(mask, columns, 0.0), axis=0, keepdims=True)


def left_right(left, right):
    lane = lax.broadcasted_iota(jnp.int32, (left.shape[0], LANES), 1)
    return jnp.where(lane < LANES // 2, left, right)


def to_words(values):
    return jnp.round(values).astype(jnp.int32).astype(jnp.int16)


def from_words(words):
    return words.astype(jnp.int32).astype(jnp.float32)


def suffix_kernel(
    len_ref, query_ref, keys_hbm, values_hbm, new_keys_ref, new_values_ref, out_ref, aux_ref, keys_ref, values_ref, sem
):
    owned, slots, _ = keys_ref.shape
    steps = new_keys_ref.shape[1]
    rows = steps * GROUP
    loads = {}
    for n in range(owned):
        for side, (source, target) in enumerate(((keys_hbm, keys_ref), (values_hbm, values_ref))):
            for part in range(LOAD_PARTS):
                span = pl.ds(part * (slots // LOAD_PARTS), slots // LOAD_PARTS)
                load = pltpu.make_async_copy(
                    source.at[n, span], target.at[n, span], sem.at[n, side, part]
                )
                load.start()
                loads.setdefault((n, side), []).append(load)
    aux = [None] * KEY_VALUE_HEADS
    for n in range(owned):
        mask = diagonal(rows, n * rows)
        for load in loads[n, 0]:
            load.wait()
        scores = []
        for h in range(KEY_VALUE_HEADS):
            columns = slice(h * HEAD_SIZE, (h + 1) * HEAD_SIZE)
            query = query_ref[h, n * rows : (n + 1) * rows, :]
            cache = contract(query, keys_ref[n, :, columns], ((1,), (1,))) * SCALING
            fresh = contract(query, new_keys_ref[n, :, columns], ((1,), (1,))) * SCALING
            cache_live = lax.broadcasted_iota(jnp.int32, cache.shape, 1) < len_ref[n]
            fresh_live = (
                lax.broadcasted_iota(jnp.int32, fresh.shape, 1)
                <= lax.broadcasted_iota(jnp.int32, fresh.shape, 0) % steps
            )
            peak = jnp.maximum(
                jnp.max(jnp.where(cache_live, cache, -jnp.inf), axis=1, keepdims=True),
                jnp.max(jnp.where(fresh_live, fresh, -jnp.inf), axis=1, keepdims=True),
            )
            cache_exp = jnp.where(cache_live, jnp.exp(cache - peak), 0.0)
            fresh_exp = jnp.where(fresh_live, jnp.exp(fresh - peak), 0.0)
            total = jnp.sum(cache_exp, axis=1, keepdims=True) + jnp.sum(
                fresh_exp, axis=1, keepdims=True
            )
            row = diagonal_row(left_right(peak, total), mask)
            aux[h] = row if aux[h] is None else aux[h] + row
            scores.append((cache_exp.astype(jnp.bfloat16), fresh_exp.astype(jnp.bfloat16)))
        for load in loads[n, 1]:
            load.wait()
        for h in range(KEY_VALUE_HEADS):
            columns = slice(h * HEAD_SIZE, (h + 1) * HEAD_SIZE)
            cache_exp, fresh_exp = scores[h]
            out_ref[h, n * rows : (n + 1) * rows, :] = contract(
                cache_exp, values_ref[n, :, columns], ((1,), (0,))
            ) + contract(fresh_exp, new_values_ref[n, :, columns], ((1,), (0,)))
    for h in range(KEY_VALUE_HEADS):
        aux_ref[h] = aux[h]


def suffix_part(suffix_len, packed, keys, values, new_keys, new_values):
    owned, _, _ = keys.shape
    rows = owned * new_keys.shape[1] * GROUP
    return pl.pallas_call(
        suffix_kernel,
        out_shape=[
            jax.ShapeDtypeStruct((KEY_VALUE_HEADS, rows, HEAD_SIZE), jnp.float32),
            jax.ShapeDtypeStruct((KEY_VALUE_HEADS, 1, LANES), jnp.float32),
        ],
        in_specs=[whole(pltpu.SMEM), whole()]
        + [whole(pltpu.HBM)] * 2
        + [whole()] * 2,
        out_specs=[whole()] * 2,
        scratch_shapes=[
            pltpu.VMEM(keys.shape, keys.dtype),
            pltpu.VMEM(values.shape, values.dtype),
            pltpu.SemaphoreType.DMA((owned, 2, LOAD_PARTS)),
        ],
        compiler_params=LIMIT,
        name="suffix_part",
    )(suffix_len, packed, keys, values, new_keys, new_values)


def attend(query, pieces, prompt, state):
    scores = [contract(query, piece[0, prompt], ((1,), (1,))) for piece in pieces]
    peaks = [jnp.max(score, axis=1, keepdims=True) for score in scores]
    weights = [jnp.exp2((score - peak) * WEIGHT_SCALE) for score, peak in zip(scores, peaks)]
    parts = [
        contract(weight.astype(jnp.bfloat16), piece[1, prompt], ((1,), (0,)))
        for weight, piece in zip(weights, pieces)
    ]
    totals = [jnp.sum(weight, axis=1, keepdims=True) for weight in weights]
    shape = parts[0].shape
    tops = [jnp.broadcast_to(peak * SCALING, shape) for peak in peaks]
    masses = [jnp.broadcast_to(total, shape) for total in totals]
    if state is not None:
        tops.append(state[0])
        masses.append(state[1])
        parts.append(state[2])
    top = functools.reduce(jnp.maximum, tops)
    factors = [jnp.exp(t - top) for t in tops]
    mass = functools.reduce(jnp.add, [m * f for m, f in zip(masses, factors)])
    out = functools.reduce(jnp.add, [p * f for p, f in zip(parts, factors)])
    return top, mass, out


def find_places(ids, prompts, rows):
    samples = ids.shape[0]
    order = jnp.arange(samples, dtype=jnp.int32)
    earlier = (ids[None, :] == ids[:, None]) & (order[None, :] < order[:, None])
    rank = jnp.sum(earlier.astype(jnp.int32), axis=1)
    return (ids * (samples // prompts) + rank) * rows


def first_kernel(rows, chunk, place_ref, queries_ref, *refs):
    pieces, refs = refs[:-4], refs[-4:]
    sorted_ref, out_ref, peak_ref, total_ref = refs
    devices = queries_ref.shape[0]
    owned = place_ref.shape[0] // devices
    prompts = pieces[0].shape[1]

    def sort_one(device, carry):
        for n in range(owned):
            target = pl.ds(pl.multiple_of(place_ref[device * owned + n], rows), rows)
            sorted_ref[target, :] = queries_ref[device, n * rows : (n + 1) * rows, :]
        return carry

    lax.fori_loop(0, devices, sort_one, 0, unroll=4)
    chunks = sorted_ref.shape[0] // prompts // chunk

    def step(index, carry):
        target = pl.ds(pl.multiple_of(index * chunk, chunk), chunk)
        peak, total, out = attend(sorted_ref[target, :], pieces, index // chunks, None)
        out_ref[target, :] = out
        peak_ref[target, :] = peak
        total_ref[target, :] = total
        return carry

    lax.fori_loop(0, prompts * chunks, step, 0, unroll=2)


def next_kernel(chunk, sorted_ref, acc_in, peak_in, total_in, *refs):
    pieces, (acc_ref, peak_ref, total_ref) = refs[:-3], refs[-3:]
    prompts = pieces[0].shape[1]
    chunks = sorted_ref.shape[0] // prompts // chunk

    def step(index, carry):
        target = pl.ds(pl.multiple_of(index * chunk, chunk), chunk)
        state = (peak_in[target, :], total_in[target, :], acc_in[target, :])
        peak, total, out = attend(sorted_ref[target, :], pieces, index // chunks, state)
        acc_ref[target, :] = out
        peak_ref[target, :] = peak
        total_ref[target, :] = total
        return carry

    lax.fori_loop(0, prompts * chunks, step, 0, unroll=2)


def last_kernel(rows, chunk, place_ref, sorted_ref, acc_ref, peak_ref, total_ref, *refs):
    pieces, refs = refs[:-3], refs[-3:]
    out_ref, out_scratch, aux_scratch = refs
    devices = out_ref.shape[0]
    owned = place_ref.shape[0] // devices
    prompts = pieces[0].shape[1]
    chunks = sorted_ref.shape[0] // prompts // chunk

    def step(index, carry):
        target = pl.ds(pl.multiple_of(index * chunk, chunk), chunk)
        state = (peak_ref[target, :], total_ref[target, :], acc_ref[target, :])
        peak, total, out = attend(sorted_ref[target, :], pieces, index // chunks, state)
        out = out / total
        largest = jnp.max(jnp.abs(out), axis=1, keepdims=True)
        code = jnp.ceil(jnp.log2(jnp.maximum(largest, TINY)) * CODE_STEPS)
        out = out * (LEVELS * jnp.exp2(code * (-1.0 / CODE_STEPS)))
        out_scratch[target, :] = to_words(jnp.clip(out, -LEVELS, LEVELS))
        aux_scratch[target, :] = left_right(peak + jnp.log(total), code)
        return carry

    lax.fori_loop(0, prompts * chunks, step, 0, unroll=2)

    mask = diagonal(owned * rows)
    first_rows = lax.broadcasted_iota(jnp.int32, (AUX_ROWS, LANES), 0) < AUX_ROWS // 2

    def emit(device, carry):
        aux_parts = []
        for n in range(owned):
            source = pl.ds(pl.multiple_of(place_ref[device * owned + n], rows), rows)
            out_ref[device, n * rows : (n + 1) * rows, :] = out_scratch[source, :]
            aux_parts.append(aux_scratch[source, :])
        row = diagonal_row(jnp.concatenate(aux_parts, axis=0), mask)
        near_part = jnp.round(row)
        rest = (row - near_part) * REST_STEPS
        words = jnp.where(first_rows, near_part, rest)
        out_ref[device, owned * rows :, :] = to_words(words)
        return carry

    lax.fori_loop(0, devices, emit, 0, unroll=4)


def first_stage(places, queries, pieces, rows):
    prompts = pieces[0].shape[1]
    total = places.shape[0] * rows
    results = pl.pallas_call(
        functools.partial(first_kernel, rows, min(512, total // prompts)),
        out_shape=[
            jax.ShapeDtypeStruct((total, HEAD_SIZE), jnp.bfloat16),
            jax.ShapeDtypeStruct((total, HEAD_SIZE), jnp.float32),
            jax.ShapeDtypeStruct((total, LANES), jnp.float32),
            jax.ShapeDtypeStruct((total, LANES), jnp.float32),
        ],
        in_specs=[whole(pltpu.SMEM)] + [whole()] * (1 + len(pieces)),
        out_specs=[whole()] * 4,
        compiler_params=LIMIT,
        name="first_stage",
    )(places, queries, *pieces)
    return [near(result) for result in results]


def next_stage(state, pieces):
    total = state[0].shape[0]
    prompts = pieces[0].shape[1]
    results = pl.pallas_call(
        functools.partial(next_kernel, min(512, total // prompts)),
        out_shape=[jax.ShapeDtypeStruct((total, HEAD_SIZE), jnp.float32)] * 3,
        in_specs=[whole()] * (4 + len(pieces)),
        out_specs=[whole()] * 3,
        compiler_params=LIMIT,
        name="next_stage",
    )(*state, *pieces)
    return [state[0]] + [near(result) for result in results]


def last_stage(places, state, pieces, rows, devices):
    prompts = pieces[0].shape[1]
    total = places.shape[0] * rows
    return pl.pallas_call(
        functools.partial(last_kernel, rows, min(512, total // prompts)),
        out_shape=jax.ShapeDtypeStruct((devices, total // devices + AUX_ROWS, HEAD_SIZE), jnp.int16),
        in_specs=[whole(pltpu.SMEM)] + [whole()] * (4 + len(pieces)),
        out_specs=whole(),
        scratch_shapes=[
            pltpu.VMEM((total, HEAD_SIZE), jnp.int16),
            pltpu.VMEM((total, HEAD_SIZE), jnp.float32),
        ],
        compiler_params=LIMIT,
        name="last_stage",
    )(places, *state, *pieces)


def merge_kernel(got_ref, local_ref, local_aux_ref, out_ref):
    owned, steps, _ = out_ref.shape
    rows = local_ref.shape[1]
    half = LANES // 2
    groups = got_ref.shape[0] // KEY_VALUE_HEADS
    local_aux = local_aux_ref[:, 0, :]
    local_total = local_aux[:, half:]
    levels = [local_aux[:, :half] + jnp.log(local_total)]
    scales = [1.0 / local_total]
    for g in range(groups):
        both = []
        for h in range(KEY_VALUE_HEADS):
            words = from_words(got_ref[g * KEY_VALUE_HEADS + h, rows:, :])
            middle = AUX_ROWS // 2
            both.append(words[:1] + words[middle : middle + 1] * (1.0 / REST_STEPS))
        aux = jnp.concatenate(both, axis=0)
        levels.append(aux[:, :half])
        scales.append(jnp.exp2(aux[:, half:] * (1.0 / CODE_STEPS)) * (1.0 / LEVELS))
    highest = functools.reduce(jnp.maximum, levels)
    weights = [jnp.exp(level - highest) for level in levels]
    denominator = functools.reduce(jnp.add, weights)
    factors = [jnp.transpose(w * s / denominator) for w, s in zip(weights, scales)]
    for h in range(KEY_VALUE_HEADS):
        result = local_ref[h] * factors[0][:, h : h + 1]
        for g in range(groups):
            part = from_words(got_ref[g * KEY_VALUE_HEADS + h, :rows, :])
            result += part * factors[g + 1][:, h : h + 1]
        for n in range(owned):
            for r in range(GROUP):
                first = (h * GROUP + r) * HEAD_SIZE
                start = (n * GROUP + r) * steps
                out_ref[n, :, first : first + HEAD_SIZE] = result[start : start + steps, :].astype(
                    jnp.bfloat16
                )


def merge(got, local, local_aux, shape):
    return pl.pallas_call(
        merge_kernel,
        out_shape=jax.ShapeDtypeStruct(shape, jnp.bfloat16),
        in_specs=[whole()] * 3,
        out_specs=whole(),
        compiler_params=LIMIT,
        name="merge",
    )(got, local, local_aux)


def body(
    queries,
    step_keys,
    step_values,
    sample_keys,
    sample_values,
    suffix_len,
    prompt_id,
    document_keys,
    document_values,
):
    owned, steps, _ = queries.shape
    devices = lax.axis_size("seq")
    rows = steps * GROUP
    assert 2 * owned * rows == LANES and devices % KEY_VALUE_HEADS == 0
    arrived = {}

    def exchange(piece, partner):
        route = [(i, i ^ partner) for i in range(devices)]
        arrived[partner] = near(lax.ppermute(piece, "seq", route))

    slices = head_slices(document_keys, document_values, FIRST)
    exchange(slices[0], FIRST[0])
    slices, packed = slices_and_queries(
        document_keys, document_values, EARLY, queries, prompt_id, devices
    )
    for partner, piece in zip(EARLY, slices):
        exchange(piece, partner)
    head_queries = lax.all_to_all(packed, "seq", split_axis=0, concat_axis=0, tiled=True)
    slices = head_slices(document_keys, document_values, LATE + (0,))
    arrived[0] = near(slices[-1])
    for partner, piece in zip(LATE, slices):
        exchange(piece, partner)
    head_ids = head_queries[:, owned * rows, :owned].reshape(-1).astype(jnp.int32)
    places = find_places(head_ids, document_keys.shape[0], rows)
    ready = [arrived[k] for k in (0, 6, 7, 1, 4, 2)]
    state = first_stage(places, near(head_queries), ready, rows)
    state = next_stage(state, [arrived[3]])
    sent = last_stage(places, state, [arrived[5]], rows, devices)
    local, local_aux = suffix_part(
        suffix_len, packed, far(sample_keys), far(sample_values), step_keys, step_values
    )
    got = near(lax.all_to_all(sent, "seq", split_axis=0, concat_axis=0, tiled=True))
    return merge(got, near(local), near(local_aux), queries.shape)


def solution(mesh):
    shared = P(("groups", "seq"), None, None)
    split = P("groups", "seq", None)
    return jax.shard_map(
        body,
        mesh=mesh,
        in_specs=(shared,) * 5 + (P(("groups", "seq")),) * 2 + (split,) * 2,
        out_specs=shared,
        check_vma=False,
    )
```

```python
import functools
import math

import jax
import jax.numpy as jnp
from jax import lax
from jax.experimental import pallas as pl
from jax.experimental.pallas import tpu as pltpu
from jax.sharding import PartitionSpec as P


QUERY_HEADS = 64
KEY_VALUE_HEADS = 8
HEAD_SIZE = 128
GROUP = QUERY_HEADS // KEY_VALUE_HEADS
SCALING = HEAD_SIZE ** (-0.5)
LANES = 128
FIRST = (6,)
EARLY = (7, 2)
SOON = (4,)
LATE = (5, 3, 1)
LIMIT = pltpu.CompilerParams(vmem_limit_bytes=24 * 1024 * 1024)
LEVELS = 32767.0
CODE_STEPS = 256.0
REST_STEPS = 65000.0
TINY = 2.0**-100
AUX_ROWS = 8
LOAD_PARTS = 4
WEIGHT_SCALE = SCALING * math.log2(math.e)


def whole(space=pltpu.VMEM):
    return pl.BlockSpec(memory_space=space)


def near(array):
    return pltpu.with_memory_space_constraint(array, pltpu.VMEM)


def far(array):
    return pltpu.with_memory_space_constraint(array, pltpu.HBM)


def start_slices(partners, keys_ref, values_ref, out_refs, sem):
    mine = lax.axis_index("seq") % KEY_VALUE_HEADS
    copies = []
    for slot, partner in enumerate(partners):
        head = jnp.bitwise_xor(mine, partner)
        columns = pl.ds(pl.multiple_of(head * HEAD_SIZE, HEAD_SIZE), HEAD_SIZE)
        for side, source in enumerate((keys_ref, values_ref)):
            copy = pltpu.make_async_copy(
                source.at[:, :, columns], out_refs[slot].at[side], sem.at[slot, side]
            )
            copy.start()
            copies.append(copy)
    return copies


def slice_kernel(partners, keys_ref, values_ref, *refs):
    for copy in start_slices(partners, keys_ref, values_ref, refs[:-1], refs[-1]):
        copy.wait()


def head_slices(keys, values, partners):
    prompts, block, _ = keys.shape
    piece = jax.ShapeDtypeStruct((2, prompts, block, HEAD_SIZE), keys.dtype)
    pieces = pl.pallas_call(
        functools.partial(slice_kernel, partners),
        out_shape=[piece] * len(partners),
        in_specs=[whole(pltpu.HBM)] * 2,
        out_specs=[whole()] * len(partners),
        scratch_shapes=[pltpu.SemaphoreType.DMA((len(partners), 2))],
        compiler_params=LIMIT,
        name="head_slices",
    )(far(keys), far(values))
    return pieces


def pack_rows(ids_ref, queries_ref, out_ref):
    owned, steps, _ = queries_ref.shape
    rows = owned * steps * GROUP
    lane = lax.broadcasted_iota(jnp.int32, (out_ref.shape[1] - rows, LANES), 1)
    marks = jnp.zeros(lane.shape, jnp.float32)
    for n in range(owned):
        marks = jnp.where(lane == n, ids_ref[n].astype(jnp.float32), marks)
    marks = marks.astype(jnp.bfloat16)
    for head in range(KEY_VALUE_HEADS):
        parts = []
        for n in range(owned):
            for r in range(GROUP):
                first = (head * GROUP + r) * HEAD_SIZE
                parts.append(queries_ref[n, :, first : first + HEAD_SIZE].astype(jnp.float32))
        block = jnp.concatenate(parts, axis=0).astype(jnp.bfloat16)
        for copy in range(out_ref.shape[0] // KEY_VALUE_HEADS):
            out_ref[copy * KEY_VALUE_HEADS + head, :rows, :] = block
            out_ref[copy * KEY_VALUE_HEADS + head, rows:, :] = marks


def slice_and_pack_kernel(partners, keys_ref, values_ref, ids_ref, queries_ref, *refs):
    out_refs, packed_ref, query_buffer, sem, query_sem = refs[:-4], *refs[-4:]
    load = pltpu.make_async_copy(queries_ref, query_buffer, query_sem)
    load.start()
    copies = start_slices(partners, keys_ref, values_ref, out_refs, sem)
    load.wait()
    pack_rows(ids_ref, query_buffer, packed_ref)
    for copy in copies:
        copy.wait()


def slices_and_queries(keys, values, partners, queries, prompt_id, devices):
    prompts, block, _ = keys.shape
    owned, steps, _ = queries.shape
    piece = jax.ShapeDtypeStruct((2, prompts, block, HEAD_SIZE), keys.dtype)
    rows = owned * steps * GROUP + AUX_ROWS
    results = pl.pallas_call(
        functools.partial(slice_and_pack_kernel, partners),
        out_shape=[piece] * len(partners)
        + [jax.ShapeDtypeStruct((devices, rows, HEAD_SIZE), jnp.bfloat16)],
        in_specs=[whole(pltpu.HBM)] * 2 + [whole(pltpu.SMEM), whole(pltpu.HBM)],
        out_specs=[whole()] * (len(partners) + 1),
        scratch_shapes=[
            pltpu.VMEM(queries.shape, queries.dtype),
            pltpu.SemaphoreType.DMA((len(partners), 2)),
            pltpu.SemaphoreType.DMA,
        ],
        compiler_params=LIMIT,
        name="slices_and_queries",
    )(far(keys), far(values), far(prompt_id), far(queries))
    return results[:-1], results[-1]


def contract(left, right, dims):
    return lax.dot_general(left, right, (dims, ((), ())), preferred_element_type=jnp.float32)


def diagonal(rows, shift=0):
    row = lax.broadcasted_iota(jnp.int32, (rows, LANES), 0) + shift
    lane = lax.broadcasted_iota(jnp.int32, (rows, LANES), 1)
    return (lane == row) | (lane == row + LANES // 2)


def diagonal_row(columns, mask):
    return jnp.sum(jnp.where(mask, columns, 0.0), axis=0, keepdims=True)


def left_right(left, right):
    lane = lax.broadcasted_iota(jnp.int32, (left.shape[0], LANES), 1)
    return jnp.where(lane < LANES // 2, left, right)


def to_words(values):
    return jnp.round(values).astype(jnp.int32).astype(jnp.int16)


def from_words(words):
    return words.astype(jnp.int32).astype(jnp.float32)


def suffix_kernel(
    len_ref, query_ref, keys_hbm, values_hbm, new_keys_ref, new_values_ref, out_ref, aux_ref, keys_ref, values_ref, sem
):
    owned, slots, _ = keys_ref.shape
    steps = new_keys_ref.shape[1]
    rows = steps * GROUP
    loads = {}
    for n in range(owned):
        for side, (source, target) in enumerate(((keys_hbm, keys_ref), (values_hbm, values_ref))):
            for part in range(LOAD_PARTS):
                span = pl.ds(part * (slots // LOAD_PARTS), slots // LOAD_PARTS)
                load = pltpu.make_async_copy(
                    source.at[n, span], target.at[n, span], sem.at[n, side, part]
                )
                load.start()
                loads.setdefault((n, side), []).append(load)
    aux = [None] * KEY_VALUE_HEADS
    for n in range(owned):
        mask = diagonal(rows, n * rows)
        for load in loads[n, 0]:
            load.wait()
        scores = []
        for h in range(KEY_VALUE_HEADS):
            columns = slice(h * HEAD_SIZE, (h + 1) * HEAD_SIZE)
            query = query_ref[h, n * rows : (n + 1) * rows, :]
            cache = contract(query, keys_ref[n, :, columns], ((1,), (1,))) * SCALING
            fresh = contract(query, new_keys_ref[n, :, columns], ((1,), (1,))) * SCALING
            cache_live = lax.broadcasted_iota(jnp.int32, cache.shape, 1) < len_ref[n]
            fresh_live = (
                lax.broadcasted_iota(jnp.int32, fresh.shape, 1)
                <= lax.broadcasted_iota(jnp.int32, fresh.shape, 0) % steps
            )
            peak = jnp.maximum(
                jnp.max(jnp.where(cache_live, cache, -jnp.inf), axis=1, keepdims=True),
                jnp.max(jnp.where(fresh_live, fresh, -jnp.inf), axis=1, keepdims=True),
            )
            cache_exp = jnp.where(cache_live, jnp.exp(cache - peak), 0.0)
            fresh_exp = jnp.where(fresh_live, jnp.exp(fresh - peak), 0.0)
            total = jnp.sum(cache_exp, axis=1, keepdims=True) + jnp.sum(
                fresh_exp, axis=1, keepdims=True
            )
            row = diagonal_row(left_right(peak, total), mask)
            aux[h] = row if aux[h] is None else aux[h] + row
            scores.append((cache_exp.astype(jnp.bfloat16), fresh_exp.astype(jnp.bfloat16)))
        for load in loads[n, 1]:
            load.wait()
        for h in range(KEY_VALUE_HEADS):
            columns = slice(h * HEAD_SIZE, (h + 1) * HEAD_SIZE)
            cache_exp, fresh_exp = scores[h]
            out_ref[h, n * rows : (n + 1) * rows, :] = contract(
                cache_exp, values_ref[n, :, columns], ((1,), (0,))
            ) + contract(fresh_exp, new_values_ref[n, :, columns], ((1,), (0,)))
    for h in range(KEY_VALUE_HEADS):
        aux_ref[h] = aux[h]


def suffix_part(suffix_len, packed, keys, values, new_keys, new_values):
    owned, _, _ = keys.shape
    rows = owned * new_keys.shape[1] * GROUP
    return pl.pallas_call(
        suffix_kernel,
        out_shape=[
            jax.ShapeDtypeStruct((KEY_VALUE_HEADS, rows, HEAD_SIZE), jnp.float32),
            jax.ShapeDtypeStruct((KEY_VALUE_HEADS, 1, LANES), jnp.float32),
        ],
        in_specs=[whole(pltpu.SMEM), whole()]
        + [whole(pltpu.HBM)] * 2
        + [whole()] * 2,
        out_specs=[whole()] * 2,
        scratch_shapes=[
            pltpu.VMEM(keys.shape, keys.dtype),
            pltpu.VMEM(values.shape, values.dtype),
            pltpu.SemaphoreType.DMA((owned, 2, LOAD_PARTS)),
        ],
        compiler_params=LIMIT,
        name="suffix_part",
    )(suffix_len, packed, keys, values, new_keys, new_values)


def attend(query, pieces, prompt, state):
    scores = [contract(query, piece[0, prompt], ((1,), (1,))) for piece in pieces]
    peaks = [jnp.max(score, axis=1, keepdims=True) for score in scores]
    weights = [jnp.exp2((score - peak) * WEIGHT_SCALE) for score, peak in zip(scores, peaks)]
    parts = [
        contract(weight.astype(jnp.bfloat16), piece[1, prompt], ((1,), (0,)))
        for weight, piece in zip(weights, pieces)
    ]
    totals = [jnp.sum(weight, axis=1, keepdims=True) for weight in weights]
    shape = parts[0].shape
    tops = [jnp.broadcast_to(peak * SCALING, shape) for peak in peaks]
    masses = [jnp.broadcast_to(total, shape) for total in totals]
    if state is not None:
        tops.append(state[0])
        masses.append(state[1])
        parts.append(state[2])
    top = functools.reduce(jnp.maximum, tops)
    factors = [jnp.exp(t - top) for t in tops]
    mass = functools.reduce(jnp.add, [m * f for m, f in zip(masses, factors)])
    out = functools.reduce(jnp.add, [p * f for p, f in zip(parts, factors)])
    return top, mass, out


def find_places(ids, prompts, rows):
    samples = ids.shape[0]
    order = jnp.arange(samples, dtype=jnp.int32)
    earlier = (ids[None, :] == ids[:, None]) & (order[None, :] < order[:, None])
    rank = jnp.sum(earlier.astype(jnp.int32), axis=1)
    return (ids * (samples // prompts) + rank) * rows


def first_kernel(rows, chunk, place_ref, queries_ref, *refs):
    pieces, refs = refs[:-4], refs[-4:]
    sorted_ref, out_ref, peak_ref, total_ref = refs
    devices = queries_ref.shape[0]
    owned = place_ref.shape[0] // devices
    prompts = pieces[0].shape[1]

    def sort_one(device, carry):
        for n in range(owned):
            target = pl.ds(pl.multiple_of(place_ref[device * owned + n], rows), rows)
            sorted_ref[target, :] = queries_ref[device, n * rows : (n + 1) * rows, :]
        return carry

    lax.fori_loop(0, devices, sort_one, 0, unroll=4)
    chunks = sorted_ref.shape[0] // prompts // chunk

    def step(index, carry):
        target = pl.ds(pl.multiple_of(index * chunk, chunk), chunk)
        peak, total, out = attend(sorted_ref[target, :], pieces, index // chunks, None)
        out_ref[target, :] = out
        peak_ref[target, :] = peak
        total_ref[target, :] = total
        return carry

    lax.fori_loop(0, prompts * chunks, step, 0, unroll=2)


def next_kernel(chunk, sorted_ref, acc_in, peak_in, total_in, *refs):
    pieces, (acc_ref, peak_ref, total_ref) = refs[:-3], refs[-3:]
    prompts = pieces[0].shape[1]
    chunks = sorted_ref.shape[0] // prompts // chunk

    def step(index, carry):
        target = pl.ds(pl.multiple_of(index * chunk, chunk), chunk)
        state = (peak_in[target, :], total_in[target, :], acc_in[target, :])
        peak, total, out = attend(sorted_ref[target, :], pieces, index // chunks, state)
        acc_ref[target, :] = out
        peak_ref[target, :] = peak
        total_ref[target, :] = total
        return carry

    lax.fori_loop(0, prompts * chunks, step, 0, unroll=2)


def last_kernel(rows, chunk, place_ref, sorted_ref, acc_ref, peak_ref, total_ref, *refs):
    pieces, refs = refs[:-3], refs[-3:]
    out_ref, out_scratch, aux_scratch = refs
    devices = out_ref.shape[0]
    owned = place_ref.shape[0] // devices
    prompts = pieces[0].shape[1]
    chunks = sorted_ref.shape[0] // prompts // chunk

    def step(index, carry):
        target = pl.ds(pl.multiple_of(index * chunk, chunk), chunk)
        state = (peak_ref[target, :], total_ref[target, :], acc_ref[target, :])
        peak, total, out = attend(sorted_ref[target, :], pieces, index // chunks, state)
        out = out / total
        largest = jnp.max(jnp.abs(out), axis=1, keepdims=True)
        code = jnp.ceil(jnp.log2(jnp.maximum(largest, TINY)) * CODE_STEPS)
        out = out * (LEVELS * jnp.exp2(code * (-1.0 / CODE_STEPS)))
        out_scratch[target, :] = to_words(jnp.clip(out, -LEVELS, LEVELS))
        aux_scratch[target, :] = left_right(peak + jnp.log(total), code)
        return carry

    lax.fori_loop(0, prompts * chunks, step, 0, unroll=2)

    mask = diagonal(owned * rows)
    first_rows = lax.broadcasted_iota(jnp.int32, (AUX_ROWS, LANES), 0) < AUX_ROWS // 2

    def emit(device, carry):
        aux_parts = []
        for n in range(owned):
            source = pl.ds(pl.multiple_of(place_ref[device * owned + n], rows), rows)
            out_ref[device, n * rows : (n + 1) * rows, :] = out_scratch[source, :]
            aux_parts.append(aux_scratch[source, :])
        row = diagonal_row(jnp.concatenate(aux_parts, axis=0), mask)
        near_part = jnp.round(row)
        rest = (row - near_part) * REST_STEPS
        words = jnp.where(first_rows, near_part, rest)
        out_ref[device, owned * rows :, :] = to_words(words)
        return carry

    lax.fori_loop(0, devices, emit, 0, unroll=4)


def first_stage(places, queries, pieces, rows):
    prompts = pieces[0].shape[1]
    total = places.shape[0] * rows
    results = pl.pallas_call(
        functools.partial(first_kernel, rows, min(512, total // prompts)),
        out_shape=[
            jax.ShapeDtypeStruct((total, HEAD_SIZE), jnp.bfloat16),
            jax.ShapeDtypeStruct((total, HEAD_SIZE), jnp.float32),
            jax.ShapeDtypeStruct((total, LANES), jnp.float32),
            jax.ShapeDtypeStruct((total, LANES), jnp.float32),
        ],
        in_specs=[whole(pltpu.SMEM)] + [whole()] * (1 + len(pieces)),
        out_specs=[whole()] * 4,
        compiler_params=LIMIT,
        name="first_stage",
    )(places, queries, *pieces)
    return [near(result) for result in results]


def next_stage(state, pieces):
    total = state[0].shape[0]
    prompts = pieces[0].shape[1]
    results = pl.pallas_call(
        functools.partial(next_kernel, min(512, total // prompts)),
        out_shape=[jax.ShapeDtypeStruct((total, HEAD_SIZE), jnp.float32)] * 3,
        in_specs=[whole()] * (4 + len(pieces)),
        out_specs=[whole()] * 3,
        compiler_params=LIMIT,
        name="next_stage",
    )(*state, *pieces)
    return [state[0]] + [near(result) for result in results]


def last_stage(places, state, pieces, rows, devices):
    prompts = pieces[0].shape[1]
    total = places.shape[0] * rows
    return pl.pallas_call(
        functools.partial(last_kernel, rows, min(512, total // prompts)),
        out_shape=jax.ShapeDtypeStruct((devices, total // devices + AUX_ROWS, HEAD_SIZE), jnp.int16),
        in_specs=[whole(pltpu.SMEM)] + [whole()] * (4 + len(pieces)),
        out_specs=whole(),
        scratch_shapes=[
            pltpu.VMEM((total, HEAD_SIZE), jnp.int16),
            pltpu.VMEM((total, HEAD_SIZE), jnp.float32),
        ],
        compiler_params=LIMIT,
        name="last_stage",
    )(places, *state, *pieces)


def merge_kernel(got_ref, local_ref, local_aux_ref, out_ref):
    owned, steps, _ = out_ref.shape
    rows = local_ref.shape[1]
    half = LANES // 2
    groups = got_ref.shape[0] // KEY_VALUE_HEADS
    local_aux = local_aux_ref[:, 0, :]
    local_total = local_aux[:, half:]
    levels = [local_aux[:, :half] + jnp.log(local_total)]
    scales = [1.0 / local_total]
    for g in range(groups):
        both = []
        for h in range(KEY_VALUE_HEADS):
            words = from_words(got_ref[g * KEY_VALUE_HEADS + h, rows:, :])
            middle = AUX_ROWS // 2
            both.append(words[:1] + words[middle : middle + 1] * (1.0 / REST_STEPS))
        aux = jnp.concatenate(both, axis=0)
        levels.append(aux[:, :half])
        scales.append(jnp.exp2(aux[:, half:] * (1.0 / CODE_STEPS)) * (1.0 / LEVELS))
    highest = functools.reduce(jnp.maximum, levels)
    weights = [jnp.exp(level - highest) for level in levels]
    denominator = functools.reduce(jnp.add, weights)
    factors = [jnp.transpose(w * s / denominator) for w, s in zip(weights, scales)]
    for h in range(KEY_VALUE_HEADS):
        result = local_ref[h] * factors[0][:, h : h + 1]
        for g in range(groups):
            part = from_words(got_ref[g * KEY_VALUE_HEADS + h, :rows, :])
            result += part * factors[g + 1][:, h : h + 1]
        for n in range(owned):
            for r in range(GROUP):
                first = (h * GROUP + r) * HEAD_SIZE
                start = (n * GROUP + r) * steps
                out_ref[n, :, first : first + HEAD_SIZE] = result[start : start + steps, :].astype(
                    jnp.bfloat16
                )


def merge(got, local, local_aux, shape):
    return pl.pallas_call(
        merge_kernel,
        out_shape=jax.ShapeDtypeStruct(shape, jnp.bfloat16),
        in_specs=[whole()] * 3,
        out_specs=whole(),
        compiler_params=LIMIT,
        name="merge",
    )(got, local, local_aux)


def body(
    queries,
    step_keys,
    step_values,
    sample_keys,
    sample_values,
    suffix_len,
    prompt_id,
    document_keys,
    document_values,
):
    owned, steps, _ = queries.shape
    devices = lax.axis_size("seq")
    rows = steps * GROUP
    assert 2 * owned * rows == LANES and devices % KEY_VALUE_HEADS == 0
    arrived = {}

    def exchange(piece, partner):
        route = [(i, i ^ partner) for i in range(devices)]
        arrived[partner] = near(lax.ppermute(piece, "seq", route))

    slices = head_slices(document_keys, document_values, FIRST)
    exchange(slices[0], FIRST[0])
    slices, packed = slices_and_queries(
        document_keys, document_values, EARLY, queries, prompt_id, devices
    )
    for partner, piece in zip(EARLY, slices):
        exchange(piece, partner)
    head_queries = lax.all_to_all(packed, "seq", split_axis=0, concat_axis=0, tiled=True)
    soon = head_slices(document_keys, document_values, SOON)
    for partner, piece in zip(SOON, soon):
        exchange(piece, partner)
    slices = head_slices(document_keys, document_values, LATE + (0,))
    arrived[0] = near(slices[-1])
    for partner, piece in zip(LATE, slices):
        exchange(piece, partner)
    head_ids = head_queries[:, owned * rows, :owned].reshape(-1).astype(jnp.int32)
    places = find_places(head_ids, document_keys.shape[0], rows)
    ready = [arrived[k] for k in (0, 6, 7, 1, 2)]
    state = first_stage(places, near(head_queries), ready, rows)
    state = next_stage(state, [arrived[k] for k in (4,)])
    sent = last_stage(places, state, [arrived[k] for k in (5, 3)], rows, devices)
    local, local_aux = suffix_part(
        suffix_len, packed, far(sample_keys), far(sample_values), step_keys, step_values
    )
    got = near(lax.all_to_all(sent, "seq", split_axis=0, concat_axis=0, tiled=True))
    return merge(got, near(local), near(local_aux), queries.shape)


def solution(mesh):
    shared = P(("groups", "seq"), None, None)
    split = P("groups", "seq", None)
    return jax.shard_map(
        body,
        mesh=mesh,
        in_specs=(shared,) * 5 + (P(("groups", "seq")),) * 2 + (split,) * 2,
        out_specs=shared,
        check_vma=False,
    )
```

```python
import functools
import math

import jax
import jax.numpy as jnp
from jax import lax
from jax.experimental import pallas as pl
from jax.experimental.pallas import tpu as pltpu
from jax.sharding import PartitionSpec as P


QUERY_HEADS = 64
KEY_VALUE_HEADS = 8
HEAD_SIZE = 128
GROUP = QUERY_HEADS // KEY_VALUE_HEADS
SCALING = HEAD_SIZE ** (-0.5)
LANES = 128
FIRST = (6,)
EARLY = (7, 2)
SOON = (4,)
LATE = (5, 3, 1)
LIMIT = pltpu.CompilerParams(vmem_limit_bytes=24 * 1024 * 1024)
LEVELS = 32767.0
CODE_STEPS = 256.0
REST_STEPS = 65000.0
TINY = 2.0**-100
AUX_ROWS = 8
LOAD_PARTS = 4
PACKED = pltpu.CompilerParams(vmem_limit_bytes=24 * 1024 * 1024)
WEIGHT_SCALE = SCALING * math.log2(math.e)


def whole(space=pltpu.VMEM):
    return pl.BlockSpec(memory_space=space)


def near(array):
    return pltpu.with_memory_space_constraint(array, pltpu.VMEM)


def far(array):
    return pltpu.with_memory_space_constraint(array, pltpu.HBM)


def start_slices(partners, keys_ref, values_ref, out_refs, sem):
    mine = lax.axis_index("seq") % KEY_VALUE_HEADS
    copies = []
    for slot, partner in enumerate(partners):
        head = jnp.bitwise_xor(mine, partner)
        columns = pl.ds(pl.multiple_of(head * HEAD_SIZE, HEAD_SIZE), HEAD_SIZE)
        for side, source in enumerate((keys_ref, values_ref)):
            copy = pltpu.make_async_copy(
                source.at[:, :, columns], out_refs[slot].at[side], sem.at[slot, side]
            )
            copy.start()
            copies.append(copy)
    return copies


def slice_kernel(partners, keys_ref, values_ref, *refs):
    for copy in start_slices(partners, keys_ref, values_ref, refs[:-1], refs[-1]):
        copy.wait()


def head_slices(keys, values, partners):
    prompts, block, _ = keys.shape
    piece = jax.ShapeDtypeStruct((2, prompts, block, HEAD_SIZE), keys.dtype)
    pieces = pl.pallas_call(
        functools.partial(slice_kernel, partners),
        out_shape=[piece] * len(partners),
        in_specs=[whole(pltpu.HBM)] * 2,
        out_specs=[whole()] * len(partners),
        scratch_shapes=[pltpu.SemaphoreType.DMA((len(partners), 2))],
        compiler_params=LIMIT,
        name="head_slices",
    )(far(keys), far(values))
    return pieces


def pack_rows(ids_ref, queries_ref, out_ref):
    owned, steps, _ = queries_ref.shape
    rows = owned * steps * GROUP
    lane = lax.broadcasted_iota(jnp.int32, (out_ref.shape[1] - rows, LANES), 1)
    marks = jnp.zeros(lane.shape, jnp.float32)
    for n in range(owned):
        marks = jnp.where(lane == n, ids_ref[n].astype(jnp.float32), marks)
    marks = marks.astype(jnp.bfloat16)
    for head in range(KEY_VALUE_HEADS):
        parts = []
        for n in range(owned):
            for r in range(GROUP):
                first = (head * GROUP + r) * HEAD_SIZE
                parts.append(queries_ref[n, :, first : first + HEAD_SIZE].astype(jnp.float32))
        block = jnp.concatenate(parts, axis=0).astype(jnp.bfloat16)
        for copy in range(out_ref.shape[0] // KEY_VALUE_HEADS):
            out_ref[copy * KEY_VALUE_HEADS + head, :rows, :] = block
            out_ref[copy * KEY_VALUE_HEADS + head, rows:, :] = marks


def slice_and_pack_kernel(partners, keys_ref, values_ref, ids_ref, queries_ref, *refs):
    out_refs, packed_ref, query_buffer, sem, query_sem = refs[:-4], *refs[-4:]
    load = pltpu.make_async_copy(queries_ref, query_buffer, query_sem)
    load.start()
    copies = start_slices(partners, keys_ref, values_ref, out_refs, sem)
    load.wait()
    pack_rows(ids_ref, query_buffer, packed_ref)
    for copy in copies:
        copy.wait()


def slices_and_queries(keys, values, partners, queries, prompt_id, devices):
    prompts, block, _ = keys.shape
    owned, steps, _ = queries.shape
    piece = jax.ShapeDtypeStruct((2, prompts, block, HEAD_SIZE), keys.dtype)
    rows = owned * steps * GROUP + AUX_ROWS
    results = pl.pallas_call(
        functools.partial(slice_and_pack_kernel, partners),
        out_shape=[piece] * len(partners)
        + [jax.ShapeDtypeStruct((devices, rows, HEAD_SIZE), jnp.bfloat16)],
        in_specs=[whole(pltpu.HBM)] * 2 + [whole(pltpu.SMEM), whole(pltpu.HBM)],
        out_specs=[whole()] * (len(partners) + 1),
        scratch_shapes=[
            pltpu.VMEM(queries.shape, queries.dtype),
            pltpu.SemaphoreType.DMA((len(partners), 2)),
            pltpu.SemaphoreType.DMA,
        ],
        compiler_params=LIMIT,
        name="slices_and_queries",
    )(far(keys), far(values), far(prompt_id), far(queries))
    return results[:-1], results[-1]


def contract(left, right, dims):
    return lax.dot_general(left, right, (dims, ((), ())), preferred_element_type=jnp.float32)


def diagonal(rows, shift=0):
    row = lax.broadcasted_iota(jnp.int32, (rows, LANES), 0) + shift
    lane = lax.broadcasted_iota(jnp.int32, (rows, LANES), 1)
    return (lane == row) | (lane == row + LANES // 2)


def diagonal_row(columns, mask):
    return jnp.sum(jnp.where(mask, columns, 0.0), axis=0, keepdims=True)


def left_right(left, right):
    lane = lax.broadcasted_iota(jnp.int32, (left.shape[0], LANES), 1)
    return jnp.where(lane < LANES // 2, left, right)


def to_words(values):
    return jnp.round(values).astype(jnp.int32).astype(jnp.int16)


def from_words(words):
    return words.astype(jnp.int32).astype(jnp.float32)


def suffix_kernel(
    len_ref, query_ref, keys_hbm, values_hbm, new_keys_ref, new_values_ref, out_ref, aux_ref, keys_ref, values_ref, sem
):
    owned, slots, _ = keys_ref.shape
    steps = new_keys_ref.shape[1]
    rows = steps * GROUP
    loads = {}
    for n in range(owned):
        for side, (source, target) in enumerate(((keys_hbm, keys_ref), (values_hbm, values_ref))):
            for part in range(LOAD_PARTS):
                span = pl.ds(part * (slots // LOAD_PARTS), slots // LOAD_PARTS)
                load = pltpu.make_async_copy(
                    source.at[n, span], target.at[n, span], sem.at[n, side, part]
                )
                load.start()
                loads.setdefault((n, side), []).append(load)
    aux = [None] * KEY_VALUE_HEADS
    for n in range(owned):
        mask = diagonal(rows, n * rows)
        for load in loads[n, 0]:
            load.wait()
        scores = []
        for h in range(KEY_VALUE_HEADS):
            columns = slice(h * HEAD_SIZE, (h + 1) * HEAD_SIZE)
            query = query_ref[h, n * rows : (n + 1) * rows, :]
            cache = contract(query, keys_ref[n, :, columns], ((1,), (1,))) * SCALING
            fresh = contract(query, new_keys_ref[n, :, columns], ((1,), (1,))) * SCALING
            cache_live = lax.broadcasted_iota(jnp.int32, cache.shape, 1) < len_ref[n]
            fresh_live = (
                lax.broadcasted_iota(jnp.int32, fresh.shape, 1)
                <= lax.broadcasted_iota(jnp.int32, fresh.shape, 0) % steps
            )
            peak = jnp.maximum(
                jnp.max(jnp.where(cache_live, cache, -jnp.inf), axis=1, keepdims=True),
                jnp.max(jnp.where(fresh_live, fresh, -jnp.inf), axis=1, keepdims=True),
            )
            cache_exp = jnp.where(cache_live, jnp.exp(cache - peak), 0.0)
            fresh_exp = jnp.where(fresh_live, jnp.exp(fresh - peak), 0.0)
            total = jnp.sum(cache_exp, axis=1, keepdims=True) + jnp.sum(
                fresh_exp, axis=1, keepdims=True
            )
            row = diagonal_row(left_right(peak, total), mask)
            aux[h] = row if aux[h] is None else aux[h] + row
            scores.append((cache_exp.astype(jnp.bfloat16), fresh_exp.astype(jnp.bfloat16)))
        for load in loads[n, 1]:
            load.wait()
        for h in range(KEY_VALUE_HEADS):
            columns = slice(h * HEAD_SIZE, (h + 1) * HEAD_SIZE)
            cache_exp, fresh_exp = scores[h]
            out_ref[h, n * rows : (n + 1) * rows, :] = contract(
                cache_exp, values_ref[n, :, columns], ((1,), (0,))
            ) + contract(fresh_exp, new_values_ref[n, :, columns], ((1,), (0,)))
    for h in range(KEY_VALUE_HEADS):
        aux_ref[h] = aux[h]


def suffix_part(suffix_len, packed, keys, values, new_keys, new_values):
    owned, _, _ = keys.shape
    rows = owned * new_keys.shape[1] * GROUP
    return pl.pallas_call(
        suffix_kernel,
        out_shape=[
            jax.ShapeDtypeStruct((KEY_VALUE_HEADS, rows, HEAD_SIZE), jnp.float32),
            jax.ShapeDtypeStruct((KEY_VALUE_HEADS, 1, LANES), jnp.float32),
        ],
        in_specs=[whole(pltpu.SMEM), whole()]
        + [whole(pltpu.HBM)] * 2
        + [whole()] * 2,
        out_specs=[whole()] * 2,
        scratch_shapes=[
            pltpu.VMEM(keys.shape, keys.dtype),
            pltpu.VMEM(values.shape, values.dtype),
            pltpu.SemaphoreType.DMA((owned, 2, LOAD_PARTS)),
        ],
        compiler_params=LIMIT,
        name="suffix_part",
    )(suffix_len, packed, keys, values, new_keys, new_values)


def attend(query, pieces, prompt, state):
    scores = [contract(query, piece[0, prompt], ((1,), (1,))) for piece in pieces]
    peaks = [jnp.max(score, axis=1, keepdims=True) for score in scores]
    weights = [jnp.exp2((score - peak) * WEIGHT_SCALE) for score, peak in zip(scores, peaks)]
    parts = [
        contract(weight.astype(jnp.bfloat16), piece[1, prompt], ((1,), (0,)))
        for weight, piece in zip(weights, pieces)
    ]
    totals = [jnp.sum(weight, axis=1, keepdims=True) for weight in weights]
    shape = parts[0].shape
    tops = [jnp.broadcast_to(peak * SCALING, shape) for peak in peaks]
    masses = [jnp.broadcast_to(total, shape) for total in totals]
    if state is not None:
        tops.append(state[0])
        masses.append(state[1])
        parts.append(state[2])
    top = functools.reduce(jnp.maximum, tops)
    factors = [jnp.exp(t - top) for t in tops]
    mass = functools.reduce(jnp.add, [m * f for m, f in zip(masses, factors)])
    out = functools.reduce(jnp.add, [p * f for p, f in zip(parts, factors)])
    return top, mass, out


def find_places(ids, prompts, rows):
    samples = ids.shape[0]
    order = jnp.arange(samples, dtype=jnp.int32)
    earlier = (ids[None, :] == ids[:, None]) & (order[None, :] < order[:, None])
    rank = jnp.sum(earlier.astype(jnp.int32), axis=1)
    return (ids * (samples // prompts) + rank) * rows


def first_kernel(rows, chunk, place_ref, queries_ref, *refs):
    pieces, refs = refs[:-4], refs[-4:]
    sorted_ref, out_ref, peak_ref, total_ref = refs
    devices = queries_ref.shape[0]
    owned = place_ref.shape[0] // devices
    prompts = pieces[0].shape[1]

    def sort_one(device, carry):
        for n in range(owned):
            target = pl.ds(pl.multiple_of(place_ref[device * owned + n], rows), rows)
            sorted_ref[target, :] = queries_ref[device, n * rows : (n + 1) * rows, :]
        return carry

    lax.fori_loop(0, devices, sort_one, 0, unroll=4)
    chunks = sorted_ref.shape[0] // prompts // chunk

    def step(index, carry):
        target = pl.ds(pl.multiple_of(index * chunk, chunk), chunk)
        peak, total, out = attend(sorted_ref[target, :], pieces, index // chunks, None)
        out_ref[target, :] = out
        peak_ref[target, :] = peak
        total_ref[target, :] = total
        return carry

    lax.fori_loop(0, prompts * chunks, step, 0, unroll=2)


def next_kernel(chunk, sorted_ref, acc_in, peak_in, total_in, *refs):
    pieces, (acc_ref, peak_ref, total_ref) = refs[:-3], refs[-3:]
    prompts = pieces[0].shape[1]
    chunks = sorted_ref.shape[0] // prompts // chunk

    def step(index, carry):
        target = pl.ds(pl.multiple_of(index * chunk, chunk), chunk)
        state = (peak_in[target, :], total_in[target, :], acc_in[target, :])
        peak, total, out = attend(sorted_ref[target, :], pieces, index // chunks, state)
        acc_ref[target, :] = out
        peak_ref[target, :] = peak
        total_ref[target, :] = total
        return carry

    lax.fori_loop(0, prompts * chunks, step, 0, unroll=2)


def last_kernel(rows, chunk, place_ref, sorted_ref, acc_ref, peak_ref, total_ref, *refs):
    pieces, refs = refs[:-3], refs[-3:]
    out_ref, out_scratch, aux_scratch = refs
    devices = out_ref.shape[0]
    owned = place_ref.shape[0] // devices
    prompts = pieces[0].shape[1]
    chunks = sorted_ref.shape[0] // prompts // chunk

    def step(index, carry):
        target = pl.ds(pl.multiple_of(index * chunk, chunk), chunk)
        state = (peak_ref[target, :], total_ref[target, :], acc_ref[target, :])
        peak, total, out = attend(sorted_ref[target, :], pieces, index // chunks, state)
        out = out / total
        largest = jnp.max(jnp.abs(out), axis=1, keepdims=True)
        code = jnp.ceil(jnp.log2(jnp.maximum(largest, TINY)) * CODE_STEPS)
        out = out * (LEVELS * jnp.exp2(code * (-1.0 / CODE_STEPS)))
        out_scratch[target, :] = to_words(jnp.clip(out, -LEVELS, LEVELS))
        aux_scratch[target, :] = left_right(peak + jnp.log(total), code)
        return carry

    lax.fori_loop(0, prompts * chunks, step, 0, unroll=2)

    mask = diagonal(owned * rows)
    first_rows = lax.broadcasted_iota(jnp.int32, (AUX_ROWS, LANES), 0) < AUX_ROWS // 2

    def emit(device, carry):
        aux_parts = []
        for n in range(owned):
            source = pl.ds(pl.multiple_of(place_ref[device * owned + n], rows), rows)
            out_ref[device, n * rows : (n + 1) * rows, :] = out_scratch[source, :]
            aux_parts.append(aux_scratch[source, :])
        row = diagonal_row(jnp.concatenate(aux_parts, axis=0), mask)
        near_part = jnp.round(row)
        rest = (row - near_part) * REST_STEPS
        words = jnp.where(first_rows, near_part, rest)
        out_ref[device, owned * rows :, :] = to_words(words)
        return carry

    lax.fori_loop(0, devices, emit, 0, unroll=16)


def first_stage(places, queries, pieces, rows):
    prompts = pieces[0].shape[1]
    total = places.shape[0] * rows
    results = pl.pallas_call(
        functools.partial(first_kernel, rows, min(512, total // prompts)),
        out_shape=[
            jax.ShapeDtypeStruct((total, HEAD_SIZE), jnp.bfloat16),
            jax.ShapeDtypeStruct((total, HEAD_SIZE), jnp.float32),
            jax.ShapeDtypeStruct((total, LANES), jnp.float32),
            jax.ShapeDtypeStruct((total, LANES), jnp.float32),
        ],
        in_specs=[whole(pltpu.SMEM)] + [whole()] * (1 + len(pieces)),
        out_specs=[whole()] * 4,
        compiler_params=PACKED,
        name="first_stage",
    )(places, queries, *pieces)
    return [near(result) for result in results]


def next_stage(state, pieces):
    total = state[0].shape[0]
    prompts = pieces[0].shape[1]
    results = pl.pallas_call(
        functools.partial(next_kernel, min(512, total // prompts)),
        out_shape=[jax.ShapeDtypeStruct((total, HEAD_SIZE), jnp.float32)] * 3,
        in_specs=[whole()] * (4 + len(pieces)),
        out_specs=[whole()] * 3,
        compiler_params=PACKED,
        name="next_stage",
    )(*state, *pieces)
    return [state[0]] + [near(result) for result in results]


def last_stage(places, state, pieces, rows, devices):
    prompts = pieces[0].shape[1]
    total = places.shape[0] * rows
    return pl.pallas_call(
        functools.partial(last_kernel, rows, min(512, total // prompts)),
        out_shape=jax.ShapeDtypeStruct((devices, total // devices + AUX_ROWS, HEAD_SIZE), jnp.int16),
        in_specs=[whole(pltpu.SMEM)] + [whole()] * (4 + len(pieces)),
        out_specs=whole(),
        scratch_shapes=[
            pltpu.VMEM((total, HEAD_SIZE), jnp.int16),
            pltpu.VMEM((total, HEAD_SIZE), jnp.float32),
        ],
        compiler_params=PACKED,
        name="last_stage",
    )(places, *state, *pieces)


def merge_kernel(got_ref, local_ref, local_aux_ref, out_ref):
    owned, steps, _ = out_ref.shape
    rows = local_ref.shape[1]
    half = LANES // 2
    groups = got_ref.shape[0] // KEY_VALUE_HEADS
    local_aux = local_aux_ref[:, 0, :]
    local_total = local_aux[:, half:]
    levels = [local_aux[:, :half] + jnp.log(local_total)]
    scales = [1.0 / local_total]
    for g in range(groups):
        both = []
        for h in range(KEY_VALUE_HEADS):
            words = from_words(got_ref[g * KEY_VALUE_HEADS + h, rows:, :])
            middle = AUX_ROWS // 2
            both.append(words[:1] + words[middle : middle + 1] * (1.0 / REST_STEPS))
        aux = jnp.concatenate(both, axis=0)
        levels.append(aux[:, :half])
        scales.append(jnp.exp2(aux[:, half:] * (1.0 / CODE_STEPS)) * (1.0 / LEVELS))
    highest = functools.reduce(jnp.maximum, levels)
    weights = [jnp.exp(level - highest) for level in levels]
    denominator = functools.reduce(jnp.add, weights)
    factors = [jnp.transpose(w * s / denominator) for w, s in zip(weights, scales)]
    for h in range(KEY_VALUE_HEADS):
        result = local_ref[h] * factors[0][:, h : h + 1]
        for g in range(groups):
            part = from_words(got_ref[g * KEY_VALUE_HEADS + h, :rows, :])
            result += part * factors[g + 1][:, h : h + 1]
        for n in range(owned):
            for r in range(GROUP):
                first = (h * GROUP + r) * HEAD_SIZE
                start = (n * GROUP + r) * steps
                out_ref[n, :, first : first + HEAD_SIZE] = result[start : start + steps, :].astype(
                    jnp.bfloat16
                )


def merge(got, local, local_aux, shape):
    return pl.pallas_call(
        merge_kernel,
        out_shape=jax.ShapeDtypeStruct(shape, jnp.bfloat16),
        in_specs=[whole()] * 3,
        out_specs=whole(),
        compiler_params=PACKED,
        name="merge",
    )(got, local, local_aux)


def body(
    queries,
    step_keys,
    step_values,
    sample_keys,
    sample_values,
    suffix_len,
    prompt_id,
    document_keys,
    document_values,
):
    owned, steps, _ = queries.shape
    devices = lax.axis_size("seq")
    rows = steps * GROUP
    assert 2 * owned * rows == LANES and devices % KEY_VALUE_HEADS == 0
    arrived = {}

    def exchange(piece, partner):
        route = [(i, i ^ partner) for i in range(devices)]
        arrived[partner] = near(lax.ppermute(piece, "seq", route))

    slices = head_slices(document_keys, document_values, FIRST)
    exchange(slices[0], FIRST[0])
    slices, packed = slices_and_queries(
        document_keys, document_values, EARLY, queries, prompt_id, devices
    )
    for partner, piece in zip(EARLY, slices):
        exchange(piece, partner)
    head_queries = lax.all_to_all(packed, "seq", split_axis=0, concat_axis=0, tiled=True)
    soon = head_slices(document_keys, document_values, SOON)
    for partner, piece in zip(SOON, soon):
        exchange(piece, partner)
    slices = head_slices(document_keys, document_values, LATE + (0,))
    arrived[0] = near(slices[-1])
    for partner, piece in zip(LATE, slices):
        exchange(piece, partner)
    head_ids = head_queries[:, owned * rows, :owned].reshape(-1).astype(jnp.int32)
    places = find_places(head_ids, document_keys.shape[0], rows)
    ready = [arrived[k] for k in (0, 6, 7, 1, 2)]
    state = first_stage(places, near(head_queries), ready, rows)
    state = next_stage(state, [arrived[k] for k in (4,)])
    sent = last_stage(places, state, [arrived[k] for k in (5, 3)], rows, devices)
    local, local_aux = suffix_part(
        suffix_len, packed, far(sample_keys), far(sample_values), step_keys, step_values
    )
    got = near(lax.all_to_all(sent, "seq", split_axis=0, concat_axis=0, tiled=True))
    return merge(got, near(local), near(local_aux), queries.shape)


def solution(mesh):
    shared = P(("groups", "seq"), None, None)
    split = P("groups", "seq", None)
    return jax.shard_map(
        body,
        mesh=mesh,
        in_specs=(shared,) * 5 + (P(("groups", "seq")),) * 2 + (split,) * 2,
        out_specs=shared,
        check_vma=False,
    )
```
